256 devices in a mesh: row: 16 (over x_lo, y, core), col: 16 (over x_hi, z).
Axes of the slice: x: 4 (x_hi: 2, x_lo: 2; x = x_hi * 2 + x_lo), y: 4, z: 8, core: 2. Of those that a mesh axis runs over, the one named last changes fastest.
Arguments:
- node_features: bfloat16 [65536, 256], P(('row', 'col')), may hold values from -6 to 6
- tile_values: bfloat16 [16, 16, 128, 128, 128], P('row', 'col'), may hold values from -0.09375 to 0.09375
- tile_coords: int32 [16, 16, 128, 2], P('row', 'col'), may hold values from 0 to 31, as said below
- tile_counts: int32 [16, 16], P('row', 'col'), may hold values from 32 to 128, as said below
- first_weight: bfloat16 [256, 256], replicated, may hold values from -0.375 to 0.375
- second_weight: bfloat16 [256, 128], replicated, may hold values from -0.375 to 0.375
- out_grad: bfloat16 [65536, 128], P(('row', 'col')), may hold values from -6 to 6
Outputs:
- output: bfloat16 [65536, 128], P(('row', 'col'))
- first_grad: float32 [256, 256], replicated
- second_grad: float32 [256, 128], replicated
The draws below stay inside these ranges and needn't reach their ends.
Inputs may be any that keep to these rules, and one draw needn't show every extreme that they name: `tile_counts`: each grid cell uses at least 32 slots; at least one grid cell uses all 128 in every draw. `tile_coords`: the first entry is a tile row below 32, the second a tile column below 32; within one grid cell no two slots share a position.
All inputs are finite; a program needn't handle non-finite values.
Results may differ from the reference program's by a relative error of at most 0.005.
Values may be sent and summed in bfloat16 or wider, within the bound.
A program may use at most 64 MiB of HBM per device.

```python
import math
import jax
import jax.numpy as jnp
from jax import lax

TILE = 128
FEAT = 256
HIDDEN_SIZE = 256
CLASSES = 128
NODE_DEV = 256
MAXT = 128
GRID_ROWS = 16
GRID_COLS = 16
ROW_TILES = 32
COL_TILES = 32
NODES = 65536


def draw_tile_counts(key, part):
    grid_rows = ROW_TILES * TILE // NODE_DEV
    grid_cols = COL_TILES * TILE // NODE_DEV
    count_key, place_key = jax.random.split(key)
    raw_draw = jax.random.randint(count_key, (grid_rows * grid_cols,), 0, MAXT + 1)
    counted = MAXT // 4 + 3 * raw_draw * raw_draw // (4 * MAXT)
    fullest = jax.random.randint(place_key, (), 0, grid_rows * grid_cols)
    counted = counted.at[fullest].set(MAXT)
    return counted.reshape(grid_rows, grid_cols).astype(jnp.int32)


def draw_tile_coords(key, part):
    grid_rows = ROW_TILES * TILE // NODE_DEV
    grid_cols = COL_TILES * TILE // NODE_DEV
    cell_keys = jax.random.split(jax.random.fold_in(key, 7), grid_rows * grid_cols)

    def pick_cell(cell_key):
        return jax.random.permutation(cell_key, ROW_TILES * COL_TILES)[:MAXT]
    places = jax.vmap(pick_cell)(cell_keys).astype(jnp.int32)
    coords = jnp.stack([places // COL_TILES, places % COL_TILES], axis=-1)
    return coords.reshape(grid_rows, grid_cols, MAXT, 2).astype(jnp.int32)


def level_of(own_key, dims, shards, least, largest):
    level, own = 1.0, jax.random.fold_in(own_key, 6)
    for position, shards_of in shards:
        draws = jnp.exp(jax.random.uniform(jax.random.fold_in(own, position), (shards_of,), jnp.float32, least / len(shards), largest / len(shards)))
        level = level * jnp.repeat(draws, dims[position] // shards_of).reshape([-1 if axis == position else 1 for axis in range(len(dims))])
    return level


def scatter_about(rng, extent, deviation, limit, shards=(), held_as=jnp.bfloat16):
    array = deviation * jax.random.normal(rng, extent, jnp.float32)
    if shards:
        array = array * level_of(rng, extent, shards, -0.22, 0.18)
    return jnp.clip(array, -limit, limit).astype(held_as)


def setup_inputs(seed: int = 0) -> dict:
    splits = jax.random.split(jax.random.key(seed), 8)
    return {
        "node_features": scatter_about(splits[0], (NODES, FEAT), 1.0, 6.0, ((0, 256),)),
        "tile_values": scatter_about(splits[1], (GRID_ROWS, GRID_COLS, MAXT, TILE, TILE), (TILE * TILE * MAXT // (2 * NODE_DEV)) ** -0.5, 0.09375, ((0, 16), (1, 16))),
        "tile_coords": draw_tile_coords(jax.random.fold_in(splits[7], 71), 0),
        "tile_counts": draw_tile_counts(jax.random.fold_in(splits[7], 71), 0),
        "first_weight": scatter_about(splits[4], (FEAT, HIDDEN_SIZE), FEAT ** -0.5, 0.375),
        "second_weight": scatter_about(splits[5], (HIDDEN_SIZE, CLASSES), HIDDEN_SIZE ** -0.5, 0.375),
        "out_grad": scatter_about(splits[6], (NODES, CLASSES), 1.0, 6.0, ((0, 256),)),
    }


HIGHEST = lax.Precision.HIGHEST

def forward_sum(tile_values, tile_coords, tile_counts, features):
    width = features.shape[-1]
    grid_feat = features.astype(jnp.float32).reshape(GRID_ROWS, COL_TILES, TILE, width)
    slot_ids = jnp.arange(MAXT, dtype=jnp.int32)
    row_ids = jnp.arange(ROW_TILES, dtype=jnp.int32)

    def one_row(total, pieces):
        tile_row, coord_row, count_row, source = pieces
        picked = source[coord_row[:, :, 1]]
        products = jnp.einsum('jtab,jtbw->jtaw', tile_row.astype(jnp.float32), picked, precision=HIGHEST)
        alive = slot_ids[None, :] < count_row[:, None]
        select = ((coord_row[:, :, 0][:, :, None] == row_ids[None, None, :]) & alive[:, :, None]).astype(jnp.float32)
        return (total + jnp.einsum('jtr,jtaw->jraw', select, products, precision=HIGHEST), None)
    start_sum = jnp.zeros((GRID_COLS, ROW_TILES, TILE, width), jnp.float32)
    total, unused = lax.scan(one_row, start_sum, (tile_values, tile_coords, tile_counts, grid_feat))
    total = total.reshape(GRID_COLS, GRID_ROWS, NODE_DEV, width).transpose(1, 0, 2, 3)
    return total.reshape(NODES, width)

def backward_sum(tile_values, tile_coords, tile_counts, features):
    width = features.shape[-1]
    grid_feat = features.astype(jnp.float32).reshape(GRID_ROWS, GRID_COLS, NODE_DEV, width)
    grid_feat = grid_feat.transpose(1, 0, 2, 3).reshape(GRID_COLS, ROW_TILES, TILE, width)
    slot_ids = jnp.arange(MAXT, dtype=jnp.int32)
    col_ids = jnp.arange(COL_TILES, dtype=jnp.int32)
    cell_ids = jnp.arange(GRID_COLS, dtype=jnp.int32)

    def one_row(carry, pieces):
        tile_row, coord_row, count_row = pieces
        picked = grid_feat[cell_ids[:, None], coord_row[:, :, 0]]
        products = jnp.einsum('jtab,jtaw->jtbw', tile_row.astype(jnp.float32), picked, precision=HIGHEST)
        alive = slot_ids[None, :] < count_row[:, None]
        select = ((coord_row[:, :, 1][:, :, None] == col_ids[None, None, :]) & alive[:, :, None]).astype(jnp.float32)
        return (carry, jnp.einsum('jtr,jtbw->rbw', select, products, precision=HIGHEST))
    unused, rows_out = lax.scan(one_row, jnp.zeros((), jnp.float32), (tile_values, tile_coords, tile_counts))
    return rows_out.reshape(NODES, width)

def reference(node_features, tile_values, tile_coords, tile_counts, first_weight, second_weight, out_grad):
    first_mean = forward_sum(tile_values, tile_coords, tile_counts, node_features)
    first_pre = jnp.dot(first_mean, first_weight.astype(jnp.float32), precision=HIGHEST)
    hidden_act = jax.nn.silu(first_pre).astype(jnp.bfloat16)
    second_mean = forward_sum(tile_values, tile_coords, tile_counts, hidden_act)
    output = jnp.dot(second_mean, second_weight.astype(jnp.float32), precision=HIGHEST).astype(jnp.bfloat16)
    back_sum = backward_sum(tile_values, tile_coords, tile_counts, out_grad)
    hidden_grad = jnp.dot(back_sum, second_weight.astype(jnp.float32).T, precision=HIGHEST)
    sigma = jax.nn.sigmoid(first_pre)
    pre_grad = hidden_grad * (sigma * (1.0 + first_pre * (1.0 - sigma)))
    scale = 1.0 / math.sqrt(NODES)
    first_grad = jnp.dot(first_mean.T, pre_grad, precision=HIGHEST) * scale
    second_grad = jnp.dot(hidden_act.astype(jnp.float32).T, back_sum, precision=HIGHEST) * scale
    return (output, first_grad, second_grad)
```

```python
import functools
import math

import jax
import jax.numpy as jnp
from jax import lax
from jax.experimental import pallas as pl
from jax.experimental.pallas import tpu as pltpu
from jax.sharding import PartitionSpec as P

HIGHEST = lax.Precision.HIGHEST
MESH = pl.DeviceIdType.MESH
ANY = pl.BlockSpec(memory_space=pl.ANY)
WHOLE = pl.BlockSpec(memory_space=pltpu.VMEM)
DMA = pltpu.SemaphoreType.DMA
F32 = jnp.float32
BF16 = jnp.bfloat16

Y = 4
Z = 8
CHIPS = 8
ROW = 16
COL = 16
NEAR = ((1, 2), (1, 1), (1, 3), (0, 2), (0, 1), (0, 3), (1, 0))
OWN_UP, OWN_DOWN, FAR_UP, FAR_DOWN = 0, 1, 2, 3
STEPS = (4, 3, 3, 4)
TILES_AT_ONCE = 16
GROUP = 4


def where_am_i():
    row = lax.axis_index("row")
    col = lax.axis_index("col")
    core = lax.rem(row, 2)
    chip = lax.div(row, 2)
    y = lax.rem(chip, Y)
    x_lo = lax.div(chip, Y)
    z = lax.rem(col, Z)
    x_hi = lax.div(col, Z)
    return row, col, core, x_lo, y, x_hi, z


def send(src, dst, send_sem, recv_sem, row, col):
    copy = pltpu.make_async_remote_copy(
        src_ref=src,
        dst_ref=dst,
        send_sem=send_sem,
        recv_sem=recv_sem,
        device_id=(row, col),
        device_id_type=MESH,
    )
    copy.start()
    return copy


def meet(partners):
    barrier = pltpu.get_barrier_semaphore()
    for partner in partners:
        pl.semaphore_signal(barrier, inc=1, device_id=partner, device_id_type=MESH)
    pl.semaphore_wait(barrier, len(partners))


def near_chips(x_lo, y, core):
    rows = []
    for dx, dy in NEAR:
        there_x = lax.rem(x_lo + dx, 2)
        there_y = lax.rem(y + dy, Y)
        rows.append((there_x * Y + there_y) * 2 + core)
    return rows


class ColGather:
    def __init__(self, mine, gathered, ring_send, ring_recv, far_send, far_recv):
        self.mine = mine
        self.gathered = gathered
        self.ring_send = ring_send
        self.ring_recv = ring_recv
        self.row, self.col, _, _, _, self.x_hi, self.z = where_am_i()
        self.far_send = far_send
        self.far_recv = far_recv
        self.rings = {}

    def block(self, far, z):
        x_hi = 1 - self.x_hi if far else self.x_hi
        return x_hi * Z + lax.rem(z + Z, Z)

    def ring(self, channel, step):
        up = channel in (OWN_UP, FAR_UP)
        far = channel in (FAR_UP, FAR_DOWN)
        shift = 1 if up else -1
        slot = self.block(far, self.z - shift * step)
        src = self.mine if (step == 0 and not far) else self.gathered.at[slot]
        self.rings[channel, step] = send(
            src,
            self.gathered.at[slot],
            self.ring_send.at[channel, step],
            self.ring_recv.at[channel, step],
            self.row,
            self.block(False, self.z + shift),
        )

    def start(self):
        self.exchange = send(
            self.mine,
            self.gathered.at[self.col],
            self.far_send,
            self.far_recv,
            self.row,
            self.block(True, self.z),
        )
        self.ring(OWN_UP, 0)
        self.ring(OWN_DOWN, 0)

    def pass_on(self, channel, step):
        self.rings[channel, step - 1].wait_recv()
        if step < STEPS[channel]:
            self.ring(channel, step)

    def middle(self):
        self.pass_on(OWN_UP, 1)
        self.pass_on(OWN_DOWN, 1)
        self.exchange.wait_recv()
        self.ring(FAR_UP, 0)
        self.ring(FAR_DOWN, 0)
        self.pass_on(OWN_UP, 2)
        self.pass_on(OWN_DOWN, 2)
        self.pass_on(FAR_UP, 1)
        self.pass_on(FAR_DOWN, 1)

    def last(self):
        self.pass_on(OWN_UP, 3)
        self.pass_on(OWN_DOWN, 3)
        self.pass_on(FAR_UP, 2)
        self.pass_on(FAR_DOWN, 2)
        self.pass_on(OWN_UP, 4)
        self.pass_on(FAR_UP, 3)
        self.pass_on(FAR_DOWN, 3)
        self.pass_on(FAR_DOWN, 4)
        self.exchange.wait_send()
        for copy in self.rings.values():
            copy.wait_send()


def gather_kernel(
    x_ref, g_ref, gx_ref, gg_ref,
    ring_send, ring_recv, far_sems, near_send, near_recv, pair_send, pair_recv, own_sems,
):
    row, col, core, x_lo, y, x_hi, z = where_am_i()
    rows = near_chips(x_lo, y, core)
    sibling = row + 1 - 2 * core
    gather = ColGather(x_ref, gx_ref, ring_send, ring_recv, far_sems.at[0], far_sems.at[1])
    meet(
        [(row, gather.block(False, z + 1)), (row, gather.block(False, z - 1)), (row, gather.block(True, z))]
        + [(there, col) for there in rows]
        + [(sibling, col)]
    )
    gather.start()
    own_x = pltpu.make_async_copy(x_ref, gx_ref.at[col], own_sems.at[0])
    own_x.start()
    own_g = pltpu.make_async_copy(g_ref, gg_ref.at[row], own_sems.at[1])
    own_g.start()
    to_pair = [send(g_ref, gg_ref.at[row], pair_send.at[7], pair_recv.at[7], sibling, col)]
    to_near = []
    for i, there in enumerate(rows):
        to_near.append(
            send(g_ref, gg_ref.at[row], near_send.at[i], near_recv.at[i], there, col)
        )
    gather.middle()
    for i, (dx, dy) in enumerate(NEAR):
        from_x = lax.rem(x_lo + dx, 2)
        from_y = lax.rem(y - dy + Y, Y)
        origin = (from_x * Y + from_y) * 2 + core
        to_near[i].wait_recv()
        to_pair.append(
            send(gg_ref.at[origin], gg_ref.at[origin], pair_send.at[i], pair_recv.at[i], sibling, col)
        )
    gather.last()
    for copy in to_pair:
        copy.wait_recv()
    for copy in to_pair + to_near:
        copy.wait_send()
    own_x.wait()
    own_g.wait()


def gather_inputs(x, g):
    return pl.pallas_call(
        gather_kernel,
        out_shape=(
            jax.ShapeDtypeStruct((COL,) + x.shape, x.dtype),
            jax.ShapeDtypeStruct((ROW,) + g.shape, g.dtype),
        ),
        in_specs=[ANY, ANY],
        out_specs=(ANY, ANY),
        scratch_shapes=[
            DMA((4, 4)), DMA((4, 4)), DMA((2,)),
            DMA((7,)), DMA((7,)), DMA((8,)), DMA((8,)), DMA((2,)),
        ],
        compiler_params=pltpu.CompilerParams(collective_id=0, has_side_effects=True),
        name="gather_inputs",
    )(x, g)


def both_kernel(coords, count, tiles, xg, gg, px, pb):
    step = pl.program_id(0)
    dead_row = px.shape[0] - 1

    @pl.when(step == 0)
    def _():
        px[...] = jnp.zeros_like(px)
        pb[...] = jnp.zeros_like(pb)

    @pl.when(step * TILES_AT_ONCE < count[0])
    def _():
        for first in range(0, TILES_AT_ONCE, GROUP):
            places = []
            for j in range(first, first + GROUP):
                slot = step * TILES_AT_ONCE + j
                live = slot < count[0]
                r = coords[2 * slot]
                c = coords[2 * slot + 1]
                tile = tiles[j]
                forward = jnp.dot(tile, xg[c], preferred_element_type=F32)
                back = lax.dot_general(
                    tile, gg[r], (((0,), (0,)), ((), ())), preferred_element_type=F32
                )
                places.append(
                    (jnp.where(live, r, dead_row), jnp.where(live, c, dead_row), forward, back)
                )
            for r, c, forward, back in places:
                px[r] += forward
                pb[c] += back


def one_kernel(coords, count, tiles, xg, px):
    step = pl.program_id(0)
    dead_row = px.shape[0] - 1

    @pl.when(step == 0)
    def _():
        px[...] = jnp.zeros_like(px)

    @pl.when(step * TILES_AT_ONCE < count[0])
    def _():
        for first in range(0, TILES_AT_ONCE, GROUP):
            places = []
            for j in range(first, first + GROUP):
                slot = step * TILES_AT_ONCE + j
                live = slot < count[0]
                r = coords[2 * slot]
                c = coords[2 * slot + 1]
                forward = jnp.dot(tiles[j], xg[c], preferred_element_type=F32)
                places.append((jnp.where(live, r, dead_row), forward))
            for r, forward in places:
                px[r] += forward


def propagate(kernel, coords, count, tiles, sources, name):
    slots, edge, _ = tiles.shape
    whole = lambda shape: pl.BlockSpec(shape, lambda i, *_: (0, 0, 0))
    outs = []
    for source in sources:
        outs.append((source.shape[0] + 1,) + source.shape[1:])
    return pl.pallas_call(
        kernel,
        out_shape=tuple(jax.ShapeDtypeStruct(out, F32) for out in outs),
        grid_spec=pltpu.PrefetchScalarGridSpec(
            num_scalar_prefetch=2,
            grid=(slots // TILES_AT_ONCE,),
            in_specs=[pl.BlockSpec((TILES_AT_ONCE, edge, edge), lambda i, *_: (i, 0, 0))]
            + [whole(source.shape) for source in sources],
            out_specs=tuple(whole(out) for out in outs),
        ),
        name=name,
    )(coords, count, tiles, *sources)


def halves(value):
    high = value.astype(BF16)
    return high, (value - high.astype(F32)).astype(BF16)


def wide_dot(value, weight):
    high, low = halves(value)
    return jnp.dot(high, weight, preferred_element_type=F32) + jnp.dot(
        low, weight, preferred_element_type=F32
    )


class RowReduce:
    def __init__(self, parts, held, pair_in, out_buf, in_buf, pair_send, pair_recv, near_send, near_recv, load_sems):
        self.row, self.col, self.core, self.x_lo, self.y, _, _ = where_am_i()
        self.parts, self.held, self.pair_in = parts, held, pair_in
        self.out_buf, self.in_buf = out_buf, in_buf
        self.pair_send, self.pair_recv = pair_send, pair_recv
        self.near_send, self.near_recv = near_send, near_recv
        self.load_sems = load_sems
        self.sibling = self.row + 1 - 2 * self.core
        self.rows = near_chips(self.x_lo, self.y, self.core)

    def start(self):
        self.pairs, self.loads = [], []
        for i, there in enumerate(self.rows + [self.row]):
            other = there + 1 - 2 * self.core
            self.pairs.append(
                send(
                    self.parts.at[pl.ds(2 * other, 2)], self.pair_in.at[i],
                    self.pair_send.at[i], self.pair_recv.at[i], self.sibling, self.col,
                )
            )
            load = pltpu.make_async_copy(
                self.parts.at[pl.ds(2 * there, 2)], self.held.at[i], self.load_sems.at[i]
            )
            load.start()
            self.loads.append(load)

    def spread(self):
        self.nears = []
        for i, there in enumerate(self.rows):
            self.pairs[i].wait_recv()
            self.loads[i].wait()
            self.out_buf[i] = (self.pair_in[i] + self.held[i]).astype(BF16)
            self.nears.append(
                send(
                    self.out_buf.at[i], self.in_buf.at[i],
                    self.near_send.at[i], self.near_recv.at[i], there, self.col,
                )
            )

    def finish(self):
        self.pairs[7].wait_recv()
        self.loads[7].wait()
        total = self.pair_in[7] + self.held[7]
        for i in range(7):
            self.nears[i].wait_recv()
            total = total + self.in_buf[i].astype(F32)
        return total

    def drain(self):
        for copy in self.pairs + self.nears:
            copy.wait_send()


def row_reduce_scratch(edge, width):
    return [
        pltpu.VMEM((8, 2, edge, width), F32),
        pltpu.VMEM((8, 2, edge, width), F32),
        pltpu.VMEM((7, 2, edge, width), BF16),
        pltpu.VMEM((7, 2, edge, width), BF16),
        DMA((8,)), DMA((8,)), DMA((7,)), DMA((7,)), DMA((8,)),
    ]


def middle_kernel(
    scale,
    px_ref, pb_ref, w1_ref, w2_ref,
    gh_ref, share_ref,
    held, pair_in, out_buf, in_buf, pair_send, pair_recv, near_send, near_recv, load_sems,
    back_out, back_in, back_send, back_recv, back_far_out, back_far_in, back_far_sems,
    h_buf, ring_send, ring_recv, far_sems, own_sem,
    mean_buf, pre_buf, grad_buf, grad_in, grad_send, grad_recv,
):
    row, col, core, x_lo, y, x_hi, z = where_am_i()
    reduce = RowReduce(
        px_ref, held, pair_in, out_buf, in_buf, pair_send, pair_recv, near_send, near_recv, load_sems
    )
    gather = ColGather(h_buf, gh_ref, ring_send, ring_recv, far_sems.at[0], far_sems.at[1])
    far_col = gather.block(True, z)
    up_col = gather.block(False, z + 1)
    down_col = gather.block(False, z - 1)
    others = [lax.rem(row + k, ROW) for k in range(1, ROW)]
    meet([(row, up_col), (row, down_col), (row, far_col)] + [(there, col) for there in others])
    reduce.start()

    nodes = 2 * pb_ref.shape[1]
    width = pb_ref.shape[2]

    def back_part(far, z_to):
        block = gather.block(far, z_to)
        return pb_ref[pl.ds(2 * block, 2)].reshape(nodes, width)

    backs = {}

    def back_step(channel, step):
        up = channel in (OWN_UP, FAR_UP)
        far = channel in (FAR_UP, FAR_DOWN)
        shift = 1 if up else -1
        part = back_part(far, z + shift * (STEPS[channel] - step))
        if step:
            backs[channel, step - 1].wait_recv()
            part = part + back_in[channel, step - 1].astype(F32)
        back_out[channel, step] = part.astype(BF16)
        backs[channel, step] = send(
            back_out.at[channel, step], back_in.at[channel, step],
            back_send.at[channel, step], back_recv.at[channel, step],
            row, up_col if up else down_col,
        )

    for channel in (FAR_DOWN, OWN_UP, FAR_UP, OWN_DOWN):
        back_step(channel, 0)
    reduce.spread()
    for step in (1, 2, 3):
        for channel in (FAR_DOWN, OWN_UP, FAR_UP, OWN_DOWN):
            if step < STEPS[channel]:
                back_step(channel, step)

    def back_total(far):
        total = back_part(far, z)
        for channel in (FAR_UP, FAR_DOWN) if far else (OWN_UP, OWN_DOWN):
            step = STEPS[channel] - 1
            backs[channel, step].wait_recv()
            total = total + back_in[channel, step].astype(F32)
        return total

    back_far_out[...] = back_total(True).astype(BF16)
    back_far = send(
        back_far_out, back_far_in, back_far_sems.at[0], back_far_sems.at[1], row, far_col
    )

    mean = reduce.finish().reshape(nodes, px_ref.shape[2])
    mean_buf[...] = mean
    pre = wide_dot(mean, w1_ref[...])
    pre_buf[...] = pre
    hidden = pre * (1.0 / (1.0 + jnp.exp(-pre)))
    h_buf[...] = wide_dot(hidden, w2_ref[...]).astype(BF16)
    gather.start()
    own = pltpu.make_async_copy(h_buf, gh_ref.at[col], own_sem)
    own.start()

    back_own = back_total(False)
    back_far.wait_recv()
    back = back_own + back_far_in[...].astype(F32)
    hidden_grad = lax.dot_general(
        back, w2_ref[...].astype(F32), (((1,), (1,)), ((), ())),
        precision=HIGHEST, preferred_element_type=F32,
    )
    pre = pre_buf[...]
    sigma = 1.0 / (1.0 + jnp.exp(-pre))
    pre_grad = hidden_grad * (sigma * (1.0 + pre * (1.0 - sigma)))
    contract = (((0,), (0,)), ((), ()))
    second = lax.dot_general(
        pre * sigma, back, contract, precision=HIGHEST, preferred_element_type=F32
    )
    first = lax.dot_general(
        mean_buf[...], pre_grad, contract, precision=HIGHEST, preferred_element_type=F32
    )
    wide = first.shape[0]
    grad_buf[0:wide] = first[:, :width] * scale
    grad_buf[wide : 2 * wide] = first[:, width:] * scale
    grad_buf[2 * wide : 3 * wide] = second * scale
    share = grad_buf.shape[0] // ROW

    gather.middle()
    grads = []
    for k, there in enumerate(others):
        grads.append(
            send(
                grad_buf.at[pl.ds(there * share, share)], grad_in.at[k],
                grad_send.at[k], grad_recv.at[k], there, col,
            )
        )
    gather.last()
    total = grad_buf[pl.ds(row * share, share)]
    for k, copy in enumerate(grads):
        copy.wait_recv()
        total = total + grad_in[k]
    share_ref[...] = total
    reduce.drain()
    for copy in list(backs.values()) + [back_far] + grads:
        copy.wait_send()
    own.wait()


def middle(px, pb, w1, w2, scale):
    edge, wide = px.shape[1:]
    width = pb.shape[2]
    nodes = 2 * edge
    grad_rows = 3 * wide
    share = grad_rows // ROW
    return pl.pallas_call(
        functools.partial(middle_kernel, scale),
        out_shape=(
            jax.ShapeDtypeStruct((COL, nodes, width), BF16),
            jax.ShapeDtypeStruct((share, width), F32),
        ),
        in_specs=[ANY, WHOLE, WHOLE, WHOLE],
        out_specs=(ANY, WHOLE),
        scratch_shapes=row_reduce_scratch(edge, wide)
        + [
            pltpu.VMEM((4, 4, nodes, width), BF16),
            pltpu.VMEM((4, 4, nodes, width), BF16),
            DMA((4, 4)), DMA((4, 4)),
            pltpu.VMEM((nodes, width), BF16),
            pltpu.VMEM((nodes, width), BF16),
            DMA((2,)),
            pltpu.VMEM((nodes, width), BF16),
            DMA((4, 4)), DMA((4, 4)), DMA((2,)), DMA,
            pltpu.VMEM((nodes, wide), F32),
            pltpu.VMEM((nodes, wide), F32),
            pltpu.VMEM((grad_rows, width), F32),
            pltpu.VMEM((ROW - 1, share, width), F32),
            DMA((ROW - 1,)), DMA((ROW - 1,)),
        ],
        compiler_params=pltpu.CompilerParams(collective_id=1, has_side_effects=True),
        name="middle",
    )(px, pb, w1, w2)


def last_kernel(
    ps_ref, share_ref,
    out_ref, grad_ref,
    held, pair_in, out_buf, in_buf, pair_send, pair_recv, near_send, near_recv, load_sems,
    col_in, col_send, col_recv, own_sem, sum_buf, row_send, row_recv,
):
    row, col, core, x_lo, y, x_hi, z = where_am_i()
    reduce = RowReduce(
        ps_ref, held, pair_in, out_buf, in_buf, pair_send, pair_recv, near_send, near_recv, load_sems
    )
    rows = [lax.rem(row + k, ROW) for k in range(1, ROW)]
    cols = [lax.rem(col + k, COL) for k in range(1, COL)]
    meet([(there, col) for there in rows] + [(row, there) for there in cols])
    reduce.start()
    own = pltpu.make_async_copy(share_ref, col_in.at[col], own_sem)
    own.start()
    across = []
    for k, there in enumerate(cols):
        across.append(
            send(share_ref, col_in.at[col], col_send.at[k], col_recv.at[k], row, there)
        )
    reduce.spread()
    own.wait()
    for copy in across:
        copy.wait_recv()
    total = col_in[0]
    for k in range(1, COL):
        total = total + col_in[k]
    sum_buf[...] = total
    share = share_ref.shape[0]
    mine = pl.ds(row * share, share)
    grad_ref[mine] = total
    along = []
    for k, there in enumerate(rows):
        along.append(
            send(sum_buf, grad_ref.at[mine], row_send.at[k], row_recv.at[k], there, col)
        )
    out_ref[...] = reduce.finish().reshape(out_ref.shape).astype(out_ref.dtype)
    for copy in along:
        copy.wait_recv()
    reduce.drain()
    for copy in across + along:
        copy.wait_send()


def last(ps, share):
    edge, width = ps.shape[1:]
    return pl.pallas_call(
        last_kernel,
        out_shape=(
            jax.ShapeDtypeStruct((2 * edge, width), BF16),
            jax.ShapeDtypeStruct((ROW * share.shape[0], width), F32),
        ),
        in_specs=[ANY, WHOLE],
        out_specs=(WHOLE, WHOLE),
        scratch_shapes=row_reduce_scratch(edge, width)
        + [
            pltpu.VMEM((COL,) + share.shape, F32),
            DMA((COL - 1,)), DMA((COL - 1,)), DMA,
            pltpu.VMEM(share.shape, F32),
            DMA((ROW - 1,)), DMA((ROW - 1,)),
        ],
        compiler_params=pltpu.CompilerParams(collective_id=2, has_side_effects=True),
        name="last",
    )(ps, share)


def on_device(
    node_features, tile_values, tile_coords, tile_counts, first_weight, second_weight, out_grad
):
    edge = tile_values.shape[-1]
    slots = tile_values.shape[2]
    tiles = tile_values.reshape(slots, edge, edge)
    coords = tile_coords.reshape(2 * slots)
    count = tile_counts.reshape(1)
    scale = 1.0 / math.sqrt(node_features.shape[0] * ROW * COL)
    gx, gg = gather_inputs(node_features, out_grad)
    px, pb = propagate(
        both_kernel, coords, count, tiles,
        [gx.reshape(-1, edge, gx.shape[-1]), gg.reshape(-1, edge, gg.shape[-1])], "both",
    )
    gh, share = middle(px, pb, first_weight, second_weight, scale)
    (ps,) = propagate(
        one_kernel, coords, count, tiles, [gh.reshape(-1, edge, gh.shape[-1])], "one"
    )
    output, grads = last(ps, share)
    wide = first_weight.shape[0]
    first_grad = jnp.concatenate([grads[:wide], grads[wide : 2 * wide]], axis=1)
    return (output, first_grad, grads[2 * wide :])


def solution(mesh):
    return jax.shard_map(
        on_device,
        mesh=mesh,
        in_specs=(
            P(("row", "col"), None),
            P("row", "col", None, None, None),
            P("row", "col", None, None),
            P("row", "col"),
            P(),
            P(),
            P(("row", "col"), None),
        ),
        out_specs=(P(("row", "col"), None), P(), P()),
        check_vma=False,
    )
```

```python
import functools
import math

import jax
import jax.numpy as jnp
from jax import lax
from jax.experimental import pallas as pl
from jax.experimental.pallas import tpu as pltpu
from jax.sharding import PartitionSpec as P

HIGHEST = lax.Precision.HIGHEST
MESH = pl.DeviceIdType.MESH
ANY = pl.BlockSpec(memory_space=pl.ANY)
WHOLE = pl.BlockSpec(memory_space=pltpu.VMEM)
DMA = pltpu.SemaphoreType.DMA
F32 = jnp.float32
BF16 = jnp.bfloat16

Y = 4
Z = 8
CHIPS = 8
ROW = 16
COL = 16
NEAR = ((1, 2), (1, 1), (1, 3), (0, 2), (0, 1), (0, 3), (1, 0))
OWN_UP, OWN_DOWN, FAR_UP, FAR_DOWN = 0, 1, 2, 3
STEPS = (4, 3, 3, 4)
TILES_AT_ONCE = 16
GROUP = 4


def where_am_i():
    row = lax.axis_index("row")
    col = lax.axis_index("col")
    core = lax.rem(row, 2)
    chip = lax.div(row, 2)
    y = lax.rem(chip, Y)
    x_lo = lax.div(chip, Y)
    z = lax.rem(col, Z)
    x_hi = lax.div(col, Z)
    return row, col, core, x_lo, y, x_hi, z


def send(src, dst, send_sem, recv_sem, row, col):
    copy = pltpu.make_async_remote_copy(
        src_ref=src,
        dst_ref=dst,
        send_sem=send_sem,
        recv_sem=recv_sem,
        device_id=(row, col),
        device_id_type=MESH,
    )
    copy.start()
    return copy


def meet(partners):
    barrier = pltpu.get_barrier_semaphore()
    for partner in partners:
        pl.semaphore_signal(barrier, inc=1, device_id=partner, device_id_type=MESH)
    pl.semaphore_wait(barrier, len(partners))


def near_chips(x_lo, y, core):
    rows = []
    for dx, dy in NEAR:
        there_x = lax.rem(x_lo + dx, 2)
        there_y = lax.rem(y + dy, Y)
        rows.append((there_x * Y + there_y) * 2 + core)
    return rows


class ColGather:
    def __init__(self, mine, gathered, ring_send, ring_recv, far_send, far_recv):
        self.mine = mine
        self.gathered = gathered
        self.ring_send = ring_send
        self.ring_recv = ring_recv
        self.row, self.col, _, _, _, self.x_hi, self.z = where_am_i()
        self.far_send = far_send
        self.far_recv = far_recv
        self.pieces = far_send.shape[0]
        self.size = mine.shape[0] // self.pieces
        self.rings = {}
        self.exchange = []

    def block(self, far, z):
        x_hi = 1 - self.x_hi if far else self.x_hi
        return x_hi * Z + lax.rem(z + Z, Z)

    def ring(self, channel, step, piece):
        up = channel in (OWN_UP, FAR_UP)
        far = channel in (FAR_UP, FAR_DOWN)
        shift = 1 if up else -1
        slot = self.block(far, self.z - shift * step)
        rows = pl.ds(piece * self.size, self.size)
        there = self.gathered.at[slot, rows]
        self.rings[channel, step, piece] = send(
            self.mine.at[rows] if (step == 0 and not far) else there,
            there,
            self.ring_send.at[channel, step, piece],
            self.ring_recv.at[channel, step, piece],
            self.row,
            self.block(False, self.z + shift),
        )

    def start(self):
        for piece in range(self.pieces):
            rows = pl.ds(piece * self.size, self.size)
            self.exchange.append(
                send(
                    self.mine.at[rows],
                    self.gathered.at[self.col, rows],
                    self.far_send.at[piece],
                    self.far_recv.at[piece],
                    self.row,
                    self.block(True, self.z),
                )
            )
            self.ring(OWN_UP, 0, piece)
            self.ring(OWN_DOWN, 0, piece)

    def pass_on(self, channel, step, piece):
        if step <= STEPS[channel]:
            self.rings[channel, step - 1, piece].wait_recv()
        if step < STEPS[channel]:
            self.ring(channel, step, piece)

    def phase(self, number):
        for piece in range(self.pieces):
            self.pass_on(OWN_UP, number + 1, piece)
            self.pass_on(OWN_DOWN, number + 1, piece)
            if number == 0:
                self.exchange[piece].wait_recv()
                self.ring(FAR_UP, 0, piece)
                self.ring(FAR_DOWN, 0, piece)
            else:
                self.pass_on(FAR_UP, number, piece)
                self.pass_on(FAR_DOWN, number, piece)

    def drain(self):
        for copy in self.exchange + list(self.rings.values()):
            copy.wait_send()


PHASES = 5


def gather_sems(pieces):
    return [DMA((4, 4, pieces)), DMA((4, 4, pieces)), DMA((pieces,)), DMA((pieces,))]


def gather_kernel(
    x_ref, g_ref, gx_ref, gg_ref,
    ring_send, ring_recv, far_send, far_recv, near_send, near_recv, pair_send, pair_recv, own_sems,
):
    row, col, core, x_lo, y, x_hi, z = where_am_i()
    rows = near_chips(x_lo, y, core)
    sibling = row + 1 - 2 * core
    gather = ColGather(x_ref, gx_ref, ring_send, ring_recv, far_send, far_recv)
    meet(
        [(row, gather.block(False, z + 1)), (row, gather.block(False, z - 1)), (row, gather.block(True, z))]
        + [(there, col) for there in rows]
        + [(sibling, col)]
    )
    gather.start()
    own_x = pltpu.make_async_copy(x_ref, gx_ref.at[col], own_sems.at[0])
    own_x.start()
    own_g = pltpu.make_async_copy(g_ref, gg_ref.at[row], own_sems.at[1])
    own_g.start()
    to_pair = [send(g_ref, gg_ref.at[row], pair_send.at[7], pair_recv.at[7], sibling, col)]
    to_near = []
    for i, there in enumerate(rows):
        to_near.append(
            send(g_ref, gg_ref.at[row], near_send.at[i], near_recv.at[i], there, col)
        )
    gather.phase(0)
    gather.phase(1)
    for i, (dx, dy) in enumerate(NEAR):
        from_x = lax.rem(x_lo + dx, 2)
        from_y = lax.rem(y - dy + Y, Y)
        origin = (from_x * Y + from_y) * 2 + core
        to_near[i].wait_recv()
        to_pair.append(
            send(gg_ref.at[origin], gg_ref.at[origin], pair_send.at[i], pair_recv.at[i], sibling, col)
        )
    for number in range(2, PHASES):
        gather.phase(number)
    gather.drain()
    for copy in to_pair:
        copy.wait_recv()
    for copy in to_pair + to_near:
        copy.wait_send()
    own_x.wait()
    own_g.wait()


def gather_inputs(x, g):
    return pl.pallas_call(
        gather_kernel,
        out_shape=(
            jax.ShapeDtypeStruct((COL,) + x.shape, x.dtype),
            jax.ShapeDtypeStruct((ROW,) + g.shape, g.dtype),
        ),
        in_specs=[ANY, ANY],
        out_specs=(ANY, ANY),
        scratch_shapes=[
            *gather_sems(2),
            DMA((7,)), DMA((7,)), DMA((8,)), DMA((8,)), DMA((2,)),
        ],
        compiler_params=pltpu.CompilerParams(collective_id=0, has_side_effects=True),
        name="gather_inputs",
    )(x, g)


def both_kernel(coords, count, tiles, xg, gg, px, pb):
    step = pl.program_id(0)
    dead_row = px.shape[0] - 1

    @pl.when(step == 0)
    def _():
        px[...] = jnp.zeros_like(px)
        pb[...] = jnp.zeros_like(pb)

    @pl.when(step * TILES_AT_ONCE < count[0])
    def _():
        for first in range(0, TILES_AT_ONCE, GROUP):
            places = []
            for j in range(first, first + GROUP):
                slot = step * TILES_AT_ONCE + j
                live = slot < count[0]
                r = coords[0, slot]
                c = coords[1, slot]
                tile = tiles[j]
                forward = jnp.dot(tile, xg[c], preferred_element_type=F32)
                back = lax.dot_general(
                    tile, gg[r], (((0,), (0,)), ((), ())), preferred_element_type=F32
                )
                places.append(
                    (jnp.where(live, r, dead_row), jnp.where(live, c, dead_row), forward, back)
                )
            for r, c, forward, back in places:
                px[r] += forward
                pb[c] += back


def one_kernel(coords, count, tiles, xg, px):
    step = pl.program_id(0)
    dead_row = px.shape[0] - 1

    @pl.when(step == 0)
    def _():
        px[...] = jnp.zeros_like(px)

    @pl.when(step * TILES_AT_ONCE < count[0])
    def _():
        for first in range(0, TILES_AT_ONCE, GROUP):
            places = []
            for j in range(first, first + GROUP):
                slot = step * TILES_AT_ONCE + j
                live = slot < count[0]
                r = coords[0, slot]
                c = coords[1, slot]
                forward = jnp.dot(tiles[j], xg[c], preferred_element_type=F32)
                places.append((jnp.where(live, r, dead_row), forward))
            for r, forward in places:
                px[r] += forward


def propagate(kernel, coords, count, tiles, sources, name):
    slots, edge, _ = tiles.shape
    whole = lambda shape: pl.BlockSpec(shape, lambda i, *_: (0, 0, 0))
    outs = []
    for source in sources:
        outs.append((source.shape[0] + 1,) + source.shape[1:])
    return pl.pallas_call(
        kernel,
        out_shape=tuple(jax.ShapeDtypeStruct(out, F32) for out in outs),
        grid_spec=pltpu.PrefetchScalarGridSpec(
            num_scalar_prefetch=2,
            grid=(slots // TILES_AT_ONCE,),
            in_specs=[pl.BlockSpec((TILES_AT_ONCE, edge, edge), lambda i, *_: (i, 0, 0))]
            + [whole(source.shape) for source in sources],
            out_specs=tuple(whole(out) for out in outs),
        ),
        name=name,
    )(coords, count, tiles, *sources)


def halves(value):
    high = value.astype(BF16)
    return high, (value - high.astype(F32)).astype(BF16)


def wide_dot(value, weight):
    high, low = halves(value)
    return jnp.dot(high, weight, preferred_element_type=F32) + jnp.dot(
        low, weight, preferred_element_type=F32
    )


class RowReduce:
    def __init__(self, parts, held, pair_in, out_buf, in_buf, pair_send, pair_recv, near_send, near_recv, load_sems):
        self.row, self.col, self.core, self.x_lo, self.y, _, _ = where_am_i()
        self.parts, self.held, self.pair_in = parts, held, pair_in
        self.out_buf, self.in_buf = out_buf, in_buf
        self.pair_send, self.pair_recv = pair_send, pair_recv
        self.near_send, self.near_recv = near_send, near_recv
        self.load_sems = load_sems
        self.sibling = self.row + 1 - 2 * self.core
        self.rows = near_chips(self.x_lo, self.y, self.core)

    def start(self):
        self.pairs, self.loads = [], []
        for i, there in enumerate(self.rows + [self.row]):
            other = there + 1 - 2 * self.core
            self.pairs.append(
                send(
                    self.parts.at[pl.ds(2 * other, 2)], self.pair_in.at[i],
                    self.pair_send.at[i], self.pair_recv.at[i], self.sibling, self.col,
                )
            )
            load = pltpu.make_async_copy(
                self.parts.at[pl.ds(2 * there, 2)], self.held.at[i], self.load_sems.at[i]
            )
            load.start()
            self.loads.append(load)

    def spread(self):
        self.nears = []
        for i, there in enumerate(self.rows):
            self.pairs[i].wait_recv()
            self.loads[i].wait()
            self.out_buf[i] = (self.pair_in[i] + self.held[i]).astype(BF16)
            self.nears.append(
                send(
                    self.out_buf.at[i], self.in_buf.at[i],
                    self.near_send.at[i], self.near_recv.at[i], there, self.col,
                )
            )

    def finish(self):
        self.pairs[7].wait_recv()
        self.loads[7].wait()
        total = self.pair_in[7] + self.held[7]
        for i in range(7):
            self.nears[i].wait_recv()
            total = total + self.in_buf[i].astype(F32)
        return total

    def drain(self):
        for copy in self.pairs + self.nears:
            copy.wait_send()


def row_reduce_scratch(edge, width):
    return [
        pltpu.VMEM((8, 2, edge, width), F32),
        pltpu.VMEM((8, 2, edge, width), F32),
        pltpu.VMEM((7, 2, edge, width), BF16),
        pltpu.VMEM((7, 2, edge, width), BF16),
        DMA((8,)), DMA((8,)), DMA((7,)), DMA((7,)), DMA((8,)),
    ]


def middle_kernel(
    scale,
    px_ref, pb_ref, w1_ref, w2_ref,
    gh_ref, share_ref,
    held, pair_in, out_buf, in_buf, pair_send, pair_recv, near_send, near_recv, load_sems,
    back_out, back_in, back_send, back_recv, back_far_out, back_far_in, back_far_sems,
    h_buf, ring_send, ring_recv, far_send, far_recv, own_sem,
    mean_buf, pre_buf, grad_buf, grad_pair, pair_sems, half_buf, grad_in, grad_send, grad_recv,
):
    row, col, core, x_lo, y, x_hi, z = where_am_i()
    reduce = RowReduce(
        px_ref, held, pair_in, out_buf, in_buf, pair_send, pair_recv, near_send, near_recv, load_sems
    )
    gather = ColGather(h_buf, gh_ref, ring_send, ring_recv, far_send, far_recv)
    far_col = gather.block(True, z)
    up_col = gather.block(False, z + 1)
    down_col = gather.block(False, z - 1)
    partners = [(there, col) for there in [reduce.sibling] + reduce.rows]
    meet([(row, up_col), (row, down_col), (row, far_col)] + partners)
    reduce.start()

    nodes = 2 * pb_ref.shape[1]
    width = pb_ref.shape[2]

    def back_part(far, z_to):
        block = gather.block(far, z_to)
        return pb_ref[pl.ds(2 * block, 2)].reshape(nodes, width)

    backs = {}

    def back_step(channel, step):
        up = channel in (OWN_UP, FAR_UP)
        far = channel in (FAR_UP, FAR_DOWN)
        shift = 1 if up else -1
        part = back_part(far, z + shift * (STEPS[channel] - step))
        if step:
            backs[channel, step - 1].wait_recv()
            part = part + back_in[channel, step - 1].astype(F32)
        back_out[channel, step] = part.astype(BF16)
        backs[channel, step] = send(
            back_out.at[channel, step], back_in.at[channel, step],
            back_send.at[channel, step], back_recv.at[channel, step],
            row, up_col if up else down_col,
        )

    for channel in (FAR_DOWN, OWN_UP, FAR_UP, OWN_DOWN):
        back_step(channel, 0)
    reduce.spread()
    for step in (1, 2, 3):
        for channel in (FAR_DOWN, OWN_UP, FAR_UP, OWN_DOWN):
            if step < STEPS[channel]:
                back_step(channel, step)

    def back_total(far):
        total = back_part(far, z)
        for channel in (FAR_UP, FAR_DOWN) if far else (OWN_UP, OWN_DOWN):
            step = STEPS[channel] - 1
            backs[channel, step].wait_recv()
            total = total + back_in[channel, step].astype(F32)
        return total

    mean = reduce.finish().reshape(nodes, px_ref.shape[2])
    mean_buf[...] = mean
    pre = wide_dot(mean, w1_ref[...])
    pre_buf[...] = pre
    hidden = pre * (1.0 / (1.0 + jnp.exp(-pre)))
    h_buf[...] = wide_dot(hidden, w2_ref[...]).astype(BF16)
    gather.start()
    own = pltpu.make_async_copy(h_buf, gh_ref.at[col], own_sem)
    own.start()

    back_far_out[...] = back_total(True).astype(BF16)
    back_far = send(
        back_far_out, back_far_in, back_far_sems.at[0], back_far_sems.at[1], row, far_col
    )
    back_own = back_total(False)
    gather.phase(0)
    back_far.wait_recv()
    back = back_own + back_far_in[...].astype(F32)
    hidden_grad = lax.dot_general(
        back, w2_ref[...].astype(F32), (((1,), (1,)), ((), ())),
        precision=HIGHEST, preferred_element_type=F32,
    )
    pre = pre_buf[...]
    sigma = 1.0 / (1.0 + jnp.exp(-pre))
    pre_grad = hidden_grad * (sigma * (1.0 + pre * (1.0 - sigma)))
    contract = (((0,), (0,)), ((), ()))
    gather.phase(1)
    second = lax.dot_general(
        pre * sigma, back, contract, precision=HIGHEST, preferred_element_type=F32
    )
    first = lax.dot_general(
        mean_buf[...], pre_grad, contract, precision=HIGHEST, preferred_element_type=F32
    )
    wide = first.shape[0]
    grad_buf[0:wide] = first[:, :width] * scale
    grad_buf[wide : 2 * wide] = first[:, width:] * scale
    grad_buf[2 * wide : 3 * wide] = second * scale
    half = grad_buf.shape[0] // 2
    share = half // CHIPS
    pair = send(
        grad_buf.at[pl.ds((1 - core) * half, half)], grad_pair,
        pair_sems.at[0], pair_sems.at[1], reduce.sibling, col,
    )
    gather.phase(2)
    pair.wait_recv()
    half_buf[...] = grad_buf[pl.ds(core * half, half)] + grad_pair[...]
    grads = []
    for i, there in enumerate(reduce.rows):
        grads.append(
            send(
                half_buf.at[pl.ds(lax.div(there, 2) * share, share)], grad_in.at[i],
                grad_send.at[i], grad_recv.at[i], there, col,
            )
        )
    gather.phase(3)
    gather.phase(4)
    total = half_buf[pl.ds(lax.div(row, 2) * share, share)]
    for i, copy in enumerate(grads):
        copy.wait_recv()
        total = total + grad_in[i]
    share_ref[...] = total.astype(BF16)
    reduce.drain()
    gather.drain()
    for copy in list(backs.values()) + [back_far, pair] + grads:
        copy.wait_send()
    own.wait()


def middle(px, pb, w1, w2, scale):
    edge, wide = px.shape[1:]
    width = pb.shape[2]
    nodes = 2 * edge
    grad_rows = 3 * wide
    share = grad_rows // ROW
    return pl.pallas_call(
        functools.partial(middle_kernel, scale),
        out_shape=(
            jax.ShapeDtypeStruct((COL, nodes, width), BF16),
            jax.ShapeDtypeStruct((share, width), BF16),
        ),
        in_specs=[ANY, WHOLE, WHOLE, WHOLE],
        out_specs=(ANY, WHOLE),
        scratch_shapes=row_reduce_scratch(edge, wide)
        + [
            pltpu.VMEM((4, 4, nodes, width), BF16),
            pltpu.VMEM((4, 4, nodes, width), BF16),
            DMA((4, 4)), DMA((4, 4)),
            pltpu.VMEM((nodes, width), BF16),
            pltpu.VMEM((nodes, width), BF16),
            DMA((2,)),
            pltpu.VMEM((nodes, width), BF16),
            *gather_sems(2), DMA,
            pltpu.VMEM((nodes, wide), F32),
            pltpu.VMEM((nodes, wide), F32),
            pltpu.VMEM((grad_rows, width), F32),
            pltpu.VMEM((grad_rows // 2, width), F32),
            DMA((2,)),
            pltpu.VMEM((grad_rows // 2, width), F32),
            pltpu.VMEM((CHIPS - 1, share, width), F32),
            DMA((CHIPS - 1,)), DMA((CHIPS - 1,)),
        ],
        compiler_params=pltpu.CompilerParams(collective_id=1, has_side_effects=True),
        name="middle",
    )(px, pb, w1, w2)


def last_kernel(
    ps_ref, share_ref,
    out_ref, grad_ref,
    held, pair_in, out_buf, in_buf, pair_send, pair_recv, near_send, near_recv, load_sems,
    col_in, ring_send, ring_recv, far_send, far_recv, own_sem,
    sum_buf, row_send, row_recv, twin_send, twin_recv,
):
    row, col, core, x_lo, y, x_hi, z = where_am_i()
    reduce = RowReduce(
        ps_ref, held, pair_in, out_buf, in_buf, pair_send, pair_recv, near_send, near_recv, load_sems
    )
    gather = ColGather(share_ref, col_in, ring_send, ring_recv, far_send, far_recv)
    ring = [gather.block(False, z + 1), gather.block(False, z - 1), gather.block(True, z)]
    sibling = reduce.sibling
    meet([(there, col) for there in [sibling] + reduce.rows] + [(row, there) for there in ring])
    gather.start()
    reduce.start()
    own = pltpu.make_async_copy(share_ref, col_in.at[col], own_sem)
    own.start()
    reduce.spread()
    for number in range(PHASES):
        gather.phase(number)
    own.wait()
    total = col_in[0].astype(F32)
    for k in range(1, COL):
        total = total + col_in[k].astype(F32)
    sum_buf[...] = total
    share = share_ref.shape[0]

    def place(chip):
        return pl.ds((core * CHIPS + chip) * share, share)

    mine = place(lax.div(row, 2))
    grad_ref[mine] = total
    along = []
    for i, there in enumerate(reduce.rows):
        along.append(
            send(sum_buf, grad_ref.at[mine], row_send.at[i], row_recv.at[i], there, col)
        )
    twins = [send(sum_buf, grad_ref.at[mine], twin_send.at[7], twin_recv.at[7], sibling, col)]
    out_ref[...] = reduce.finish().reshape(out_ref.shape)
    for i, (dx, dy) in enumerate(NEAR):
        from_x = lax.rem(x_lo + dx, 2)
        from_y = lax.rem(y - dy + Y, Y)
        along[i].wait_recv()
        theirs = place(from_x * Y + from_y)
        twins.append(
            send(
                grad_ref.at[theirs], grad_ref.at[theirs],
                twin_send.at[i], twin_recv.at[i], sibling, col,
            )
        )
    for copy in twins:
        copy.wait_recv()
    reduce.drain()
    gather.drain()
    for copy in along + twins:
        copy.wait_send()


def last(ps, share):
    edge, width = ps.shape[1:]
    return pl.pallas_call(
        last_kernel,
        out_shape=(
            jax.ShapeDtypeStruct((2 * edge, width), F32),
            jax.ShapeDtypeStruct((ROW * share.shape[0], width), F32),
        ),
        in_specs=[ANY, WHOLE],
        out_specs=(WHOLE, WHOLE),
        scratch_shapes=row_reduce_scratch(edge, width)
        + [
            pltpu.VMEM((COL,) + share.shape, BF16),
            *gather_sems(1), DMA,
            pltpu.VMEM(share.shape, F32),
            DMA((7,)), DMA((7,)), DMA((8,)), DMA((8,)),
        ],
        compiler_params=pltpu.CompilerParams(collective_id=2, has_side_effects=True),
        name="last",
    )(ps, share)


def arrange_kernel(out_ref, grad_ref, output_ref, first_ref, second_ref):
    wide = first_ref.shape[0]
    width = second_ref.shape[1]
    output_ref[...] = out_ref[...].astype(BF16)
    first_ref[:, :width] = grad_ref[:wide]
    first_ref[:, width:] = grad_ref[wide : 2 * wide]
    second_ref[...] = grad_ref[2 * wide :]


def arrange(out, grads, wide):
    return pl.pallas_call(
        arrange_kernel,
        out_shape=(
            jax.ShapeDtypeStruct(out.shape, BF16),
            jax.ShapeDtypeStruct((wide, 2 * grads.shape[1]), F32),
            jax.ShapeDtypeStruct((wide, grads.shape[1]), F32),
        ),
        in_specs=[WHOLE, WHOLE],
        out_specs=(WHOLE, WHOLE, WHOLE),
        name="arrange",
    )(out, grads)


def on_device(
    node_features, tile_values, tile_coords, tile_counts, first_weight, second_weight, out_grad
):
    edge = tile_values.shape[-1]
    slots = tile_values.shape[2]
    tiles = tile_values.reshape(slots, edge, edge)
    coords = tile_coords.reshape(slots, 2).T
    count = tile_counts.reshape(1)
    scale = 1.0 / math.sqrt(node_features.shape[0] * ROW * COL)
    gx, gg = gather_inputs(node_features, out_grad)
    px, pb = propagate(
        both_kernel, coords, count, tiles,
        [gx.reshape(-1, edge, gx.shape[-1]), gg.reshape(-1, edge, gg.shape[-1])], "both",
    )
    gh, share = middle(px, pb, first_weight, second_weight, scale)
    (ps,) = propagate(
        one_kernel, coords, count, tiles, [gh.reshape(-1, edge, gh.shape[-1])], "one"
    )
    out, grads = last(ps, share)
    return arrange(out, grads, first_weight.shape[0])


def solution(mesh):
    return jax.shard_map(
        on_device,
        mesh=mesh,
        in_specs=(
            P(("row", "col"), None),
            P("row", "col", None, None, None),
            P("row", "col", None, None),
            P("row", "col"),
            P(),
            P(),
            P(("row", "col"), None),
        ),
        out_specs=(P(("row", "col"), None), P(), P()),
        check_vma=False,
    )
```

```python
import functools
import math

import jax
import jax.numpy as jnp
from jax import lax
from jax.experimental import pallas as pl
from jax.experimental.pallas import tpu as pltpu
from jax.sharding import PartitionSpec as P

HIGHEST = lax.Precision.HIGHEST
MESH = pl.DeviceIdType.MESH
ANY = pl.BlockSpec(memory_space=pl.ANY)
WHOLE = pl.BlockSpec(memory_space=pltpu.VMEM)
DMA = pltpu.SemaphoreType.DMA
F32 = jnp.float32
BF16 = jnp.bfloat16

Y = 4
Z = 8
CHIPS = 8
ROW = 16
COL = 16
NEAR = ((1, 2), (1, 1), (1, 3), (0, 2), (0, 1), (0, 3), (1, 0))
OWN_UP, OWN_DOWN, FAR_UP, FAR_DOWN = 0, 1, 2, 3
STEPS = (4, 3, 3, 4)
TILES_AT_ONCE = 16
SCOPED = 24 * 2**20
GROUP = 4


def where_am_i():
    row = lax.axis_index("row")
    col = lax.axis_index("col")
    core = lax.rem(row, 2)
    chip = lax.div(row, 2)
    y = lax.rem(chip, Y)
    x_lo = lax.div(chip, Y)
    z = lax.rem(col, Z)
    x_hi = lax.div(col, Z)
    return row, col, core, x_lo, y, x_hi, z


def send(src, dst, send_sem, recv_sem, row, col):
    copy = pltpu.make_async_remote_copy(
        src_ref=src,
        dst_ref=dst,
        send_sem=send_sem,
        recv_sem=recv_sem,
        device_id=(row, col),
        device_id_type=MESH,
    )
    copy.start()
    return copy


def meet(partners):
    barrier = pltpu.get_barrier_semaphore()
    for partner in partners:
        pl.semaphore_signal(barrier, inc=1, device_id=partner, device_id_type=MESH)
    pl.semaphore_wait(barrier, len(partners))


def near_chips(x_lo, y, core):
    rows = []
    for dx, dy in NEAR:
        there_x = lax.rem(x_lo + dx, 2)
        there_y = lax.rem(y + dy, Y)
        rows.append((there_x * Y + there_y) * 2 + core)
    return rows


class ColGather:
    def __init__(self, mine, gathered, ring_send, ring_recv, far_send, far_recv):
        self.mine = mine
        self.gathered = gathered
        self.ring_send = ring_send
        self.ring_recv = ring_recv
        self.row, self.col, _, _, _, self.x_hi, self.z = where_am_i()
        self.far_send = far_send
        self.far_recv = far_recv
        self.pieces = far_send.shape[0]
        self.size = mine.shape[0] // self.pieces
        self.rings = {}
        self.exchange = []

    def block(self, far, z):
        x_hi = 1 - self.x_hi if far else self.x_hi
        return x_hi * Z + lax.rem(z + Z, Z)

    def ring(self, channel, step, piece):
        up = channel in (OWN_UP, FAR_UP)
        far = channel in (FAR_UP, FAR_DOWN)
        shift = 1 if up else -1
        slot = self.block(far, self.z - shift * step)
        rows = pl.ds(piece * self.size, self.size)
        there = self.gathered.at[slot, rows]
        self.rings[channel, step, piece] = send(
            self.mine.at[rows] if (step == 0 and not far) else there,
            there,
            self.ring_send.at[channel, step, piece],
            self.ring_recv.at[channel, step, piece],
            self.row,
            self.block(False, self.z + shift),
        )

    def start(self):
        for piece in range(self.pieces):
            rows = pl.ds(piece * self.size, self.size)
            self.exchange.append(
                send(
                    self.mine.at[rows],
                    self.gathered.at[self.col, rows],
                    self.far_send.at[piece],
                    self.far_recv.at[piece],
                    self.row,
                    self.block(True, self.z),
                )
            )
            self.ring(OWN_UP, 0, piece)
            self.ring(OWN_DOWN, 0, piece)

    def pass_on(self, channel, step, piece):
        if step <= STEPS[channel]:
            self.rings[channel, step - 1, piece].wait_recv()
        if step < STEPS[channel]:
            self.ring(channel, step, piece)

    def phase(self, number):
        for piece in range(self.pieces):
            self.pass_on(OWN_UP, number + 1, piece)
            self.pass_on(OWN_DOWN, number + 1, piece)
            if number == 0:
                self.exchange[piece].wait_recv()
                self.ring(FAR_UP, 0, piece)
                self.ring(FAR_DOWN, 0, piece)
            else:
                self.pass_on(FAR_UP, number, piece)
                self.pass_on(FAR_DOWN, number, piece)

    def drain(self):
        for copy in self.exchange + list(self.rings.values()):
            copy.wait_send()


PHASES = 5


def gather_sems(pieces):
    return [DMA((4, 4, pieces)), DMA((4, 4, pieces)), DMA((pieces,)), DMA((pieces,))]


def gather_kernel(
    x_ref, g_ref, gx_ref, gg_ref,
    ring_send, ring_recv, far_send, far_recv, near_send, near_recv, pair_send, pair_recv, own_sems,
):
    row, col, core, x_lo, y, x_hi, z = where_am_i()
    rows = near_chips(x_lo, y, core)
    sibling = row + 1 - 2 * core
    gather = ColGather(x_ref, gx_ref, ring_send, ring_recv, far_send, far_recv)
    meet(
        [(row, gather.block(False, z + 1)), (row, gather.block(False, z - 1)), (row, gather.block(True, z))]
        + [(there, col) for there in rows]
        + [(sibling, col)]
    )
    gather.start()
    own_x = pltpu.make_async_copy(x_ref, gx_ref.at[col], own_sems.at[0])
    own_x.start()
    own_g = pltpu.make_async_copy(g_ref, gg_ref.at[row], own_sems.at[1])
    own_g.start()
    to_pair = [send(g_ref, gg_ref.at[row], pair_send.at[7], pair_recv.at[7], sibling, col)]
    to_near = []
    for i, there in enumerate(rows):
        to_near.append(
            send(g_ref, gg_ref.at[row], near_send.at[i], near_recv.at[i], there, col)
        )
    gather.phase(0)
    gather.phase(1)
    for i, (dx, dy) in enumerate(NEAR):
        from_x = lax.rem(x_lo + dx, 2)
        from_y = lax.rem(y - dy + Y, Y)
        origin = (from_x * Y + from_y) * 2 + core
        to_near[i].wait_recv()
        to_pair.append(
            send(gg_ref.at[origin], gg_ref.at[origin], pair_send.at[i], pair_recv.at[i], sibling, col)
        )
    for number in range(2, PHASES):
        gather.phase(number)
    gather.drain()
    for copy in to_pair:
        copy.wait_recv()
    for copy in to_pair + to_near:
        copy.wait_send()
    own_x.wait()
    own_g.wait()


def gather_inputs(x, g):
    return pl.pallas_call(
        gather_kernel,
        out_shape=(
            jax.ShapeDtypeStruct((COL,) + x.shape, x.dtype),
            jax.ShapeDtypeStruct((ROW,) + g.shape, g.dtype),
        ),
        in_specs=[ANY, ANY],
        out_specs=(ANY, ANY),
        scratch_shapes=[
            *gather_sems(2),
            DMA((7,)), DMA((7,)), DMA((8,)), DMA((8,)), DMA((2,)),
        ],
        compiler_params=pltpu.CompilerParams(collective_id=0, has_side_effects=True, vmem_limit_bytes=SCOPED),
        name="gather_inputs",
    )(x, g)


def both_kernel(coords, count, tiles, xg, gg, px, pb):
    step = pl.program_id(0)
    dead_row = px.shape[0] - 1

    @pl.when(step == 0)
    def _():
        px[...] = jnp.zeros_like(px)
        pb[...] = jnp.zeros_like(pb)

    @pl.when(step * TILES_AT_ONCE < count[0])
    def _():
        for first in range(0, TILES_AT_ONCE, GROUP):
            places = []
            for j in range(first, first + GROUP):
                slot = step * TILES_AT_ONCE + j
                live = slot < count[0]
                r = coords[0, slot]
                c = coords[1, slot]
                tile = tiles[j]
                forward = jnp.dot(tile, xg[c], preferred_element_type=F32)
                back = lax.dot_general(
                    tile, gg[r], (((0,), (0,)), ((), ())), preferred_element_type=F32
                )
                places.append(
                    (jnp.where(live, r, dead_row), jnp.where(live, c, dead_row), forward, back)
                )
            for r, c, forward, back in places:
                px[r] += forward
                pb[c] += back


def one_kernel(coords, count, tiles, xg, px):
    step = pl.program_id(0)
    dead_row = px.shape[0] - 1

    @pl.when(step == 0)
    def _():
        px[...] = jnp.zeros_like(px)

    @pl.when(step * TILES_AT_ONCE < count[0])
    def _():
        for first in range(0, TILES_AT_ONCE, GROUP):
            places = []
            for j in range(first, first + GROUP):
                slot = step * TILES_AT_ONCE + j
                live = slot < count[0]
                r = coords[0, slot]
                c = coords[1, slot]
                forward = jnp.dot(tiles[j], xg[c], preferred_element_type=F32)
                places.append((jnp.where(live, r, dead_row), forward))
            for r, forward in places:
                px[r] += forward


def propagate(kernel, coords, count, tiles, sources, name):
    slots, edge, _ = tiles.shape
    whole = lambda shape: pl.BlockSpec(shape, lambda i, *_: (0, 0, 0))
    outs = []
    for source in sources:
        outs.append((source.shape[0] + 1,) + source.shape[1:])
    return pl.pallas_call(
        kernel,
        out_shape=tuple(jax.ShapeDtypeStruct(out, F32) for out in outs),
        grid_spec=pltpu.PrefetchScalarGridSpec(
            num_scalar_prefetch=2,
            grid=(slots // TILES_AT_ONCE,),
            in_specs=[pl.BlockSpec((TILES_AT_ONCE, edge, edge), lambda i, *_: (i, 0, 0))]
            + [whole(source.shape) for source in sources],
            out_specs=tuple(whole(out) for out in outs),
        ),
        compiler_params=pltpu.CompilerParams(vmem_limit_bytes=SCOPED),
        name=name,
    )(coords, count, tiles, *sources)


def halves(value):
    high = value.astype(BF16)
    return high, (value - high.astype(F32)).astype(BF16)


def wide_dot(value, weight):
    high, low = halves(value)
    return jnp.dot(high, weight, preferred_element_type=F32) + jnp.dot(
        low, weight, preferred_element_type=F32
    )


class RowReduce:
    def __init__(self, parts, held, pair_in, out_buf, in_buf, pair_send, pair_recv, near_send, near_recv, load_sems):
        self.row, self.col, self.core, self.x_lo, self.y, _, _ = where_am_i()
        self.parts, self.held, self.pair_in = parts, held, pair_in
        self.out_buf, self.in_buf = out_buf, in_buf
        self.pair_send, self.pair_recv = pair_send, pair_recv
        self.near_send, self.near_recv = near_send, near_recv
        self.load_sems = load_sems
        self.sibling = self.row + 1 - 2 * self.core
        self.rows = near_chips(self.x_lo, self.y, self.core)

    def start(self):
        self.pairs, self.loads = [], []
        for i, there in enumerate(self.rows + [self.row]):
            other = there + 1 - 2 * self.core
            self.pairs.append(
                send(
                    self.parts.at[pl.ds(2 * other, 2)], self.pair_in.at[i],
                    self.pair_send.at[i], self.pair_recv.at[i], self.sibling, self.col,
                )
            )
            load = pltpu.make_async_copy(
                self.parts.at[pl.ds(2 * there, 2)], self.held.at[i], self.load_sems.at[i]
            )
            load.start()
            self.loads.append(load)

    def spread(self):
        self.nears = []
        for i, there in enumerate(self.rows):
            self.pairs[i].wait_recv()
            self.loads[i].wait()
            self.out_buf[i] = (self.pair_in[i] + self.held[i]).astype(BF16)
            self.nears.append(
                send(
                    self.out_buf.at[i], self.in_buf.at[i],
                    self.near_send.at[i], self.near_recv.at[i], there, self.col,
                )
            )

    def finish(self):
        self.pairs[7].wait_recv()
        self.loads[7].wait()
        total = self.pair_in[7] + self.held[7]
        for i in range(7):
            self.nears[i].wait_recv()
            total = total + self.in_buf[i].astype(F32)
        return total

    def drain(self):
        for copy in self.pairs + self.nears:
            copy.wait_send()


def row_reduce_scratch(edge, width):
    return [
        pltpu.VMEM((8, 2, edge, width), F32),
        pltpu.VMEM((8, 2, edge, width), F32),
        pltpu.VMEM((7, 2, edge, width), BF16),
        pltpu.VMEM((7, 2, edge, width), BF16),
        DMA((8,)), DMA((8,)), DMA((7,)), DMA((7,)), DMA((8,)),
    ]


def middle_kernel(
    scale,
    px_ref, pb_ref, w1_ref, w2_ref,
    gh_ref, share_ref,
    held, pair_in, out_buf, in_buf, pair_send, pair_recv, near_send, near_recv, load_sems,
    back_out, back_in, back_send, back_recv, back_far_out, back_far_in, back_far_sems,
    h_buf, ring_send, ring_recv, far_send, far_recv, own_sem,
    mean_buf, pre_buf, grad_buf, grad_pair, pair_sems, half_buf, grad_in, grad_send, grad_recv,
):
    row, col, core, x_lo, y, x_hi, z = where_am_i()
    reduce = RowReduce(
        px_ref, held, pair_in, out_buf, in_buf, pair_send, pair_recv, near_send, near_recv, load_sems
    )
    gather = ColGather(h_buf, gh_ref, ring_send, ring_recv, far_send, far_recv)
    far_col = gather.block(True, z)
    up_col = gather.block(False, z + 1)
    down_col = gather.block(False, z - 1)
    partners = [(there, col) for there in [reduce.sibling] + reduce.rows]
    meet([(row, up_col), (row, down_col), (row, far_col)] + partners)
    reduce.start()

    nodes = 2 * pb_ref.shape[1]
    width = pb_ref.shape[2]

    def back_part(far, z_to):
        block = gather.block(far, z_to)
        return pb_ref[pl.ds(2 * block, 2)].reshape(nodes, width)

    backs = {}

    def back_step(channel, step):
        up = channel in (OWN_UP, FAR_UP)
        far = channel in (FAR_UP, FAR_DOWN)
        shift = 1 if up else -1
        part = back_part(far, z + shift * (STEPS[channel] - step))
        if step:
            backs[channel, step - 1].wait_recv()
            part = part + back_in[channel, step - 1].astype(F32)
        back_out[channel, step] = part.astype(BF16)
        backs[channel, step] = send(
            back_out.at[channel, step], back_in.at[channel, step],
            back_send.at[channel, step], back_recv.at[channel, step],
            row, up_col if up else down_col,
        )

    for channel in (FAR_DOWN, OWN_UP, FAR_UP, OWN_DOWN):
        back_step(channel, 0)
    reduce.spread()
    for step in (1, 2, 3):
        for channel in (FAR_DOWN, OWN_UP, FAR_UP, OWN_DOWN):
            if step < STEPS[channel]:
                back_step(channel, step)

    def back_total(far):
        total = back_part(far, z)
        for channel in (FAR_UP, FAR_DOWN) if far else (OWN_UP, OWN_DOWN):
            step = STEPS[channel] - 1
            backs[channel, step].wait_recv()
            total = total + back_in[channel, step].astype(F32)
        return total

    mean = reduce.finish().reshape(nodes, px_ref.shape[2])
    mean_buf[...] = mean
    pre = wide_dot(mean, w1_ref[...])
    pre_buf[...] = pre
    hidden = pre * (1.0 / (1.0 + jnp.exp(-pre)))
    h_buf[...] = wide_dot(hidden, w2_ref[...]).astype(BF16)
    gather.start()
    own = pltpu.make_async_copy(h_buf, gh_ref.at[col], own_sem)
    own.start()

    back_far_out[...] = back_total(True).astype(BF16)
    back_far = send(
        back_far_out, back_far_in, back_far_sems.at[0], back_far_sems.at[1], row, far_col
    )
    back_own = back_total(False)
    gather.phase(0)
    back_far.wait_recv()
    back = back_own + back_far_in[...].astype(F32)
    hidden_grad = lax.dot_general(
        back, w2_ref[...].astype(F32), (((1,), (1,)), ((), ())),
        precision=HIGHEST, preferred_element_type=F32,
    )
    pre = pre_buf[...]
    sigma = 1.0 / (1.0 + jnp.exp(-pre))
    pre_grad = hidden_grad * (sigma * (1.0 + pre * (1.0 - sigma)))
    contract = (((0,), (0,)), ((), ()))
    gather.phase(1)
    second = lax.dot_general(
        pre * sigma, back, contract, precision=HIGHEST, preferred_element_type=F32
    )
    first = lax.dot_general(
        mean_buf[...], pre_grad, contract, precision=HIGHEST, preferred_element_type=F32
    )
    wide = first.shape[0]
    grad_buf[0:wide] = first[:, :width] * scale
    grad_buf[wide : 2 * wide] = first[:, width:] * scale
    grad_buf[2 * wide : 3 * wide] = second * scale
    half = grad_buf.shape[0] // 2
    share = half // CHIPS
    pair = send(
        grad_buf.at[pl.ds((1 - core) * half, half)], grad_pair,
        pair_sems.at[0], pair_sems.at[1], reduce.sibling, col,
    )
    gather.phase(2)
    pair.wait_recv()
    half_buf[...] = grad_buf[pl.ds(core * half, half)] + grad_pair[...]
    grads = []
    for i, there in enumerate(reduce.rows):
        grads.append(
            send(
                half_buf.at[pl.ds(lax.div(there, 2) * share, share)], grad_in.at[i],
                grad_send.at[i], grad_recv.at[i], there, col,
            )
        )
    gather.phase(3)
    gather.phase(4)
    total = half_buf[pl.ds(lax.div(row, 2) * share, share)]
    for i, copy in enumerate(grads):
        copy.wait_recv()
        total = total + grad_in[i]
    share_ref[...] = total.astype(BF16)
    reduce.drain()
    gather.drain()
    for copy in list(backs.values()) + [back_far, pair] + grads:
        copy.wait_send()
    own.wait()


def middle(px, pb, w1, w2, scale):
    edge, wide = px.shape[1:]
    width = pb.shape[2]
    nodes = 2 * edge
    grad_rows = 3 * wide
    share = grad_rows // ROW
    return pl.pallas_call(
        functools.partial(middle_kernel, scale),
        out_shape=(
            jax.ShapeDtypeStruct((COL, nodes, width), BF16),
            jax.ShapeDtypeStruct((share, width), BF16),
        ),
        in_specs=[ANY, WHOLE, WHOLE, WHOLE],
        out_specs=(ANY, WHOLE),
        scratch_shapes=row_reduce_scratch(edge, wide)
        + [
            pltpu.VMEM((4, 4, nodes, width), BF16),
            pltpu.VMEM((4, 4, nodes, width), BF16),
            DMA((4, 4)), DMA((4, 4)),
            pltpu.VMEM((nodes, width), BF16),
            pltpu.VMEM((nodes, width), BF16),
            DMA((2,)),
            pltpu.VMEM((nodes, width), BF16),
            *gather_sems(2), DMA,
            pltpu.VMEM((nodes, wide), F32),
            pltpu.VMEM((nodes, wide), F32),
            pltpu.VMEM((grad_rows, width), F32),
            pltpu.VMEM((grad_rows // 2, width), F32),
            DMA((2,)),
            pltpu.VMEM((grad_rows // 2, width), F32),
            pltpu.VMEM((CHIPS - 1, share, width), F32),
            DMA((CHIPS - 1,)), DMA((CHIPS - 1,)),
        ],
        compiler_params=pltpu.CompilerParams(collective_id=1, has_side_effects=True, vmem_limit_bytes=SCOPED),
        name="middle",
    )(px, pb, w1, w2)


def last_kernel(
    ps_ref, share_ref,
    out_ref, grad_ref,
    held, pair_in, out_buf, in_buf, pair_send, pair_recv, near_send, near_recv, load_sems,
    col_in, col_send, col_recv, own_sem,
    sum_buf, row_send, row_recv, twin_send, twin_recv,
):
    row, col, core, x_lo, y, x_hi, z = where_am_i()
    reduce = RowReduce(
        ps_ref, held, pair_in, out_buf, in_buf, pair_send, pair_recv, near_send, near_recv, load_sems
    )
    cols = [lax.rem(col + k, COL) for k in range(1, COL)]
    sibling = reduce.sibling
    meet([(there, col) for there in [sibling] + reduce.rows] + [(row, there) for there in cols])
    across = []
    for k, there in enumerate(cols):
        across.append(
            send(share_ref, col_in.at[col], col_send.at[k], col_recv.at[k], row, there)
        )
    reduce.start()
    own = pltpu.make_async_copy(share_ref, col_in.at[col], own_sem)
    own.start()
    reduce.spread()
    own.wait()
    for copy in across:
        copy.wait_recv()
    total = col_in[0].astype(F32)
    for k in range(1, COL):
        total = total + col_in[k].astype(F32)
    sum_buf[...] = total
    share = share_ref.shape[0]

    def place(chip):
        return pl.ds((core * CHIPS + chip) * share, share)

    mine = place(lax.div(row, 2))
    grad_ref[mine] = total
    along = []
    for i, there in enumerate(reduce.rows):
        along.append(
            send(sum_buf, grad_ref.at[mine], row_send.at[i], row_recv.at[i], there, col)
        )
    twins = [send(sum_buf, grad_ref.at[mine], twin_send.at[7], twin_recv.at[7], sibling, col)]
    out_ref[...] = reduce.finish().reshape(out_ref.shape)
    for i, (dx, dy) in enumerate(NEAR):
        from_x = lax.rem(x_lo + dx, 2)
        from_y = lax.rem(y - dy + Y, Y)
        along[i].wait_recv()
        theirs = place(from_x * Y + from_y)
        twins.append(
            send(
                grad_ref.at[theirs], grad_ref.at[theirs],
                twin_send.at[i], twin_recv.at[i], sibling, col,
            )
        )
    for copy in twins:
        copy.wait_recv()
    reduce.drain()
    for copy in across + along + twins:
        copy.wait_send()


def last(ps, share):
    edge, width = ps.shape[1:]
    return pl.pallas_call(
        last_kernel,
        out_shape=(
            jax.ShapeDtypeStruct((2 * edge, width), F32),
            jax.ShapeDtypeStruct((ROW * share.shape[0], width), F32),
        ),
        in_specs=[ANY, WHOLE],
        out_specs=(WHOLE, WHOLE),
        scratch_shapes=row_reduce_scratch(edge, width)
        + [
            pltpu.VMEM((COL,) + share.shape, BF16),
            DMA((COL - 1,)), DMA((COL - 1,)), DMA,
            pltpu.VMEM(share.shape, F32),
            DMA((7,)), DMA((7,)), DMA((8,)), DMA((8,)),
        ],
        compiler_params=pltpu.CompilerParams(collective_id=2, has_side_effects=True, vmem_limit_bytes=SCOPED),
        name="last",
    )(ps, share)


def arrange_kernel(out_ref, grad_ref, output_ref, first_ref, second_ref):
    wide = first_ref.shape[0]
    width = second_ref.shape[1]
    output_ref[...] = out_ref[...].astype(BF16)
    first_ref[:, :width] = grad_ref[:wide]
    first_ref[:, width:] = grad_ref[wide : 2 * wide]
    second_ref[...] = grad_ref[2 * wide :]


def arrange(out, grads, wide):
    return pl.pallas_call(
        arrange_kernel,
        out_shape=(
            jax.ShapeDtypeStruct(out.shape, BF16),
            jax.ShapeDtypeStruct((wide, 2 * grads.shape[1]), F32),
            jax.ShapeDtypeStruct((wide, grads.shape[1]), F32),
        ),
        in_specs=[WHOLE, WHOLE],
        out_specs=(WHOLE, WHOLE, WHOLE),
        compiler_params=pltpu.CompilerParams(vmem_limit_bytes=SCOPED),
        name="arrange",
    )(out, grads)


def in_hbm(array):
    return pltpu.with_memory_space_constraint(array, pltpu.HBM)


def on_device(
    node_features, tile_values, tile_coords, tile_counts, first_weight, second_weight, out_grad
):
    edge = tile_values.shape[-1]
    slots = tile_values.shape[2]
    tiles = tile_values.reshape(slots, edge, edge)
    coords = tile_coords.reshape(slots, 2).T
    count = tile_counts.reshape(1)
    scale = 1.0 / math.sqrt(node_features.shape[0] * ROW * COL)
    gx, gg = gather_inputs(in_hbm(node_features), in_hbm(out_grad))
    px, pb = propagate(
        both_kernel, coords, count, in_hbm(tiles),
        [gx.reshape(-1, edge, gx.shape[-1]), gg.reshape(-1, edge, gg.shape[-1])], "both",
    )
    gh, share = middle(px, pb, first_weight, second_weight, scale)
    (ps,) = propagate(
        one_kernel, coords, count, tiles, [gh.reshape(-1, edge, gh.shape[-1])], "one"
    )
    out, grads = last(ps, share)
    return arrange(out, grads, first_weight.shape[0])


def solution(mesh):
    return jax.shard_map(
        on_device,
        mesh=mesh,
        in_specs=(
            P(("row", "col"), None),
            P("row", "col", None, None, None),
            P("row", "col", None, None),
            P("row", "col"),
            P(),
            P(),
            P(("row", "col"), None),
        ),
        out_specs=(P(("row", "col"), None), P(), P()),
        check_vma=False,
    )
```

```python
import functools
import math

import jax
import jax.numpy as jnp
from jax import lax
from jax.experimental import pallas as pl
from jax.experimental.pallas import tpu as pltpu
from jax.sharding import PartitionSpec as P

MESH = pl.DeviceIdType.MESH
ANY = pl.BlockSpec(memory_space=pl.ANY)
WHOLE = pl.BlockSpec(memory_space=pltpu.VMEM)
DMA = pltpu.SemaphoreType.DMA
F32 = jnp.float32
BF16 = jnp.bfloat16

Y = 4
Z = 8
CHIPS = 8
ROW = 16
COL = 16
NEAR = ((1, 2), (1, 1), (1, 3), (0, 2), (0, 1), (0, 3), (1, 0))
OWN_UP, OWN_DOWN, FAR_UP, FAR_DOWN = 0, 1, 2, 3
STEPS = (4, 3, 3, 4)
TILES_AT_ONCE = 16
SCOPED = 24 * 2**20
GROUP = 4


def where_am_i():
    row = lax.axis_index("row")
    col = lax.axis_index("col")
    core = lax.rem(row, 2)
    chip = lax.div(row, 2)
    y = lax.rem(chip, Y)
    x_lo = lax.div(chip, Y)
    z = lax.rem(col, Z)
    x_hi = lax.div(col, Z)
    return row, col, core, x_lo, y, x_hi, z


def send(src, dst, send_sem, recv_sem, row, col):
    copy = pltpu.make_async_remote_copy(
        src_ref=src,
        dst_ref=dst,
        send_sem=send_sem,
        recv_sem=recv_sem,
        device_id=(row, col),
        device_id_type=MESH,
    )
    copy.start()
    return copy


def meet(partners):
    barrier = pltpu.get_barrier_semaphore()
    for partner in partners:
        pl.semaphore_signal(barrier, inc=1, device_id=partner, device_id_type=MESH)
    pl.semaphore_wait(barrier, len(partners))


def near_chips(x_lo, y, core):
    rows = []
    for dx, dy in NEAR:
        there_x = lax.rem(x_lo + dx, 2)
        there_y = lax.rem(y + dy, Y)
        rows.append((there_x * Y + there_y) * 2 + core)
    return rows


class ColGather:
    def __init__(self, mine, gathered, ring_send, ring_recv, far_send, far_recv):
        self.mine = mine
        self.gathered = gathered
        self.ring_send = ring_send
        self.ring_recv = ring_recv
        self.row, self.col, _, _, _, self.x_hi, self.z = where_am_i()
        self.far_send = far_send
        self.far_recv = far_recv
        self.pieces = far_send.shape[0]
        self.size = mine.shape[0] // self.pieces
        self.rings = {}
        self.exchange = []

    def block(self, far, z):
        x_hi = 1 - self.x_hi if far else self.x_hi
        return x_hi * Z + lax.rem(z + Z, Z)

    def ring(self, channel, step, piece):
        up = channel in (OWN_UP, FAR_UP)
        far = channel in (FAR_UP, FAR_DOWN)
        shift = 1 if up else -1
        slot = self.block(far, self.z - shift * step)
        rows = pl.ds(piece * self.size, self.size)
        row, col = self.row, self.block(False, self.z + shift)
        if far and step == 0:
            slot, col = self.block(False, self.z - shift), self.block(True, self.z)
        there = self.gathered.at[slot, rows]
        self.rings[channel, step, piece] = send(
            self.mine.at[rows] if (step == 0 and not far) else there,
            there,
            self.ring_send.at[channel, step, piece],
            self.ring_recv.at[channel, step, piece],
            row,
            col,
        )

    def start(self):
        for piece in range(self.pieces):
            rows = pl.ds(piece * self.size, self.size)
            self.exchange.append(
                send(
                    self.mine.at[rows],
                    self.gathered.at[self.col, rows],
                    self.far_send.at[piece],
                    self.far_recv.at[piece],
                    self.row,
                    self.block(True, self.z),
                )
            )
            self.ring(OWN_UP, 0, piece)
            self.ring(OWN_DOWN, 0, piece)

    def pass_on(self, channel, step, piece):
        if step <= STEPS[channel]:
            self.rings[channel, step - 1, piece].wait_recv()
        if step < STEPS[channel]:
            self.ring(channel, step, piece)

    def phase(self, number):
        for piece in range(self.pieces):
            self.pass_on(OWN_UP, number + 1, piece)
            if number == 0:
                self.ring(FAR_UP, 0, piece)
            self.pass_on(OWN_DOWN, number + 1, piece)
            if number == 0:
                self.ring(FAR_DOWN, 0, piece)
            else:
                self.pass_on(FAR_UP, number, piece)
                self.pass_on(FAR_DOWN, number, piece)

    def drain(self):
        for copy in self.exchange:
            copy.wait_recv()
        for copy in self.exchange + list(self.rings.values()):
            copy.wait_send()


PHASES = 5


def gather_sems(pieces):
    return [DMA((4, 4, pieces)), DMA((4, 4, pieces)), DMA((pieces,)), DMA((pieces,))]


def gather_kernel(
    x_ref, g_ref, tiles_ref, gx_ref, gg_ref, near_tiles_ref,
    ring_send, ring_recv, far_send, far_recv, near_send, near_recv, pair_send, pair_recv, own_sems,
):
    row, col, core, x_lo, y, x_hi, z = where_am_i()
    own_tiles = pltpu.make_async_copy(tiles_ref, near_tiles_ref, own_sems.at[2])
    own_tiles.start()
    rows = near_chips(x_lo, y, core)
    sibling = row + 1 - 2 * core
    gather = ColGather(x_ref, gx_ref, ring_send, ring_recv, far_send, far_recv)
    meet(
        [(row, gather.block(False, z + 1)), (row, gather.block(False, z - 1)), (row, gather.block(True, z))]
        + [(there, col) for there in rows]
        + [(sibling, col)]
    )
    gather.start()
    own_x = pltpu.make_async_copy(x_ref, gx_ref.at[col], own_sems.at[0])
    own_x.start()
    own_g = pltpu.make_async_copy(g_ref, gg_ref.at[row], own_sems.at[1])
    own_g.start()
    to_pair = [send(g_ref, gg_ref.at[row], pair_send.at[7], pair_recv.at[7], sibling, col)]
    to_near = []
    for i, there in enumerate(rows):
        to_near.append(
            send(g_ref, gg_ref.at[row], near_send.at[i], near_recv.at[i], there, col)
        )
    gather.phase(0)
    gather.phase(1)
    for i, (dx, dy) in enumerate(NEAR):
        from_x = lax.rem(x_lo + dx, 2)
        from_y = lax.rem(y - dy + Y, Y)
        origin = (from_x * Y + from_y) * 2 + core
        to_near[i].wait_recv()
        to_pair.append(
            send(gg_ref.at[origin], gg_ref.at[origin], pair_send.at[i], pair_recv.at[i], sibling, col)
        )
    for number in range(2, PHASES):
        gather.phase(number)
    gather.drain()
    for copy in to_pair:
        copy.wait_recv()
    for copy in to_pair + to_near:
        copy.wait_send()
    own_x.wait()
    own_g.wait()
    own_tiles.wait()


def gather_inputs(x, g, tiles):
    return pl.pallas_call(
        gather_kernel,
        out_shape=(
            jax.ShapeDtypeStruct((COL,) + x.shape, x.dtype),
            jax.ShapeDtypeStruct((ROW,) + g.shape, g.dtype),
            jax.ShapeDtypeStruct(tiles.shape, tiles.dtype),
        ),
        in_specs=[ANY, ANY, ANY],
        out_specs=(ANY, ANY, ANY),
        scratch_shapes=[
            *gather_sems(2),
            DMA((7,)), DMA((7,)), DMA((8,)), DMA((8,)), DMA((3,)),
        ],
        compiler_params=pltpu.CompilerParams(collective_id=0, has_side_effects=True, vmem_limit_bytes=SCOPED),
        name="gather_inputs",
    )(x, g, tiles)


def both_kernel(coords, count, tiles, xg, gg, px, pb):
    step = pl.program_id(0)
    dead_row = px.shape[0] - 1

    @pl.when(step == 0)
    def _():
        px[...] = jnp.zeros_like(px)
        pb[...] = jnp.zeros_like(pb)

    @pl.when(step * TILES_AT_ONCE < count[0])
    def _():
        for first in range(0, TILES_AT_ONCE, GROUP):
            places = []
            for j in range(first, first + GROUP):
                slot = step * TILES_AT_ONCE + j
                live = slot < count[0]
                r = coords[0, slot]
                c = coords[1, slot]
                tile = tiles[j]
                forward = jnp.dot(tile, xg[c], preferred_element_type=F32)
                back = lax.dot_general(
                    tile, gg[r], (((0,), (0,)), ((), ())), preferred_element_type=F32
                )
                places.append(
                    (jnp.where(live, r, dead_row), jnp.where(live, c, dead_row), forward, back)
                )
            for r, c, forward, back in places:
                px[r] += forward
                pb[c] += back


def one_kernel(coords, count, tiles, xg, px):
    step = pl.program_id(0)
    dead_row = px.shape[0] - 1

    @pl.when(step == 0)
    def _():
        px[...] = jnp.zeros_like(px)

    @pl.when(step * TILES_AT_ONCE < count[0])
    def _():
        for first in range(0, TILES_AT_ONCE, GROUP):
            places = []
            for j in range(first, first + GROUP):
                slot = step * TILES_AT_ONCE + j
                live = slot < count[0]
                r = coords[0, slot]
                c = coords[1, slot]
                forward = jnp.dot(tiles[j], xg[c], preferred_element_type=F32)
                places.append((jnp.where(live, r, dead_row), forward))
            for r, forward in places:
                px[r] += forward


def propagate(kernel, coords, count, tiles, sources, name):
    slots, edge, _ = tiles.shape
    whole = lambda shape: pl.BlockSpec(shape, lambda i, *_: (0, 0, 0))
    outs = []
    for source in sources:
        outs.append((source.shape[0] + 1,) + source.shape[1:])
    return pl.pallas_call(
        kernel,
        out_shape=tuple(jax.ShapeDtypeStruct(out, F32) for out in outs),
        grid_spec=pltpu.PrefetchScalarGridSpec(
            num_scalar_prefetch=2,
            grid=(slots // TILES_AT_ONCE,),
            in_specs=[pl.BlockSpec((TILES_AT_ONCE, edge, edge), lambda i, *_: (i, 0, 0))]
            + [whole(source.shape) for source in sources],
            out_specs=tuple(whole(out) for out in outs),
        ),
        compiler_params=pltpu.CompilerParams(vmem_limit_bytes=SCOPED),
        name=name,
    )(coords, count, tiles, *sources)


def halves(value):
    high = value.astype(BF16)
    return high, (value - high.astype(F32)).astype(BF16)


def wide_dot(value, weight):
    high, low = halves(value)
    return jnp.dot(high, weight, preferred_element_type=F32) + jnp.dot(
        low, weight, preferred_element_type=F32
    )


def split_dot(left, right, contract):
    left_high, left_low = halves(left)
    right_high, right_low = halves(right)
    total = lax.dot_general(left_high, right_high, contract, preferred_element_type=F32)
    total += lax.dot_general(left_high, right_low, contract, preferred_element_type=F32)
    total += lax.dot_general(left_low, right_high, contract, preferred_element_type=F32)
    return total


class RowReduce:
    def __init__(self, parts, held, pair_in, out_buf, in_buf, pair_send, pair_recv, near_send, near_recv, load_sems):
        self.row, self.col, self.core, self.x_lo, self.y, _, _ = where_am_i()
        self.parts, self.held, self.pair_in = parts, held, pair_in
        self.out_buf, self.in_buf = out_buf, in_buf
        self.pair_send, self.pair_recv = pair_send, pair_recv
        self.near_send, self.near_recv = near_send, near_recv
        self.load_sems = load_sems
        self.sibling = self.row + 1 - 2 * self.core
        self.rows = near_chips(self.x_lo, self.y, self.core)

    def start(self):
        self.pairs, self.loads = [], []
        for i, there in enumerate(self.rows + [self.row]):
            other = there + 1 - 2 * self.core
            self.pairs.append(
                send(
                    self.parts.at[pl.ds(2 * other, 2)], self.pair_in.at[i],
                    self.pair_send.at[i], self.pair_recv.at[i], self.sibling, self.col,
                )
            )
            load = pltpu.make_async_copy(
                self.parts.at[pl.ds(2 * there, 2)], self.held.at[i], self.load_sems.at[i]
            )
            load.start()
            self.loads.append(load)

    def spread(self):
        self.nears = []
        for i, there in enumerate(self.rows):
            self.pairs[i].wait_recv()
            self.loads[i].wait()
            self.out_buf[i] = (self.pair_in[i] + self.held[i]).astype(BF16)
            self.nears.append(
                send(
                    self.out_buf.at[i], self.in_buf.at[i],
                    self.near_send.at[i], self.near_recv.at[i], there, self.col,
                )
            )

    def finish(self):
        self.pairs[7].wait_recv()
        self.loads[7].wait()
        total = self.pair_in[7] + self.held[7]
        for i in range(7):
            self.nears[i].wait_recv()
            total = total + self.in_buf[i].astype(F32)
        return total

    def drain(self):
        for copy in self.pairs + self.nears:
            copy.wait_send()


def row_reduce_scratch(edge, width):
    return [
        pltpu.VMEM((8, 2, edge, width), F32),
        pltpu.VMEM((8, 2, edge, width), F32),
        pltpu.VMEM((7, 2, edge, width), BF16),
        pltpu.VMEM((7, 2, edge, width), BF16),
        DMA((8,)), DMA((8,)), DMA((7,)), DMA((7,)), DMA((8,)),
    ]


def middle_kernel(
    scale,
    px_ref, pb_ref, w1_ref, w2_ref,
    gh_ref, share_ref,
    held, pair_in, out_buf, in_buf, pair_send, pair_recv, near_send, near_recv, load_sems,
    back_out, back_in, back_send, back_recv, back_far_out, back_far_in, back_far_sems,
    h_buf, ring_send, ring_recv, far_send, far_recv, own_sem,
    mean_buf, pre_buf, grad_buf, grad_pair, pair_sems, half_buf, grad_in, grad_send, grad_recv,
):
    row, col, core, x_lo, y, x_hi, z = where_am_i()
    reduce = RowReduce(
        px_ref, held, pair_in, out_buf, in_buf, pair_send, pair_recv, near_send, near_recv, load_sems
    )
    gather = ColGather(h_buf, gh_ref, ring_send, ring_recv, far_send, far_recv)
    far_col = gather.block(True, z)
    up_col = gather.block(False, z + 1)
    down_col = gather.block(False, z - 1)
    partners = [(there, col) for there in [reduce.sibling] + reduce.rows]
    meet([(row, up_col), (row, down_col), (row, far_col)] + partners)
    reduce.start()

    nodes = 2 * pb_ref.shape[1]
    width = pb_ref.shape[2]

    def back_part(far, z_to):
        block = gather.block(far, z_to)
        return pb_ref[pl.ds(2 * block, 2)].reshape(nodes, width)

    backs = {}

    def back_step(channel, step):
        up = channel in (OWN_UP, FAR_UP)
        far = channel in (FAR_UP, FAR_DOWN)
        shift = 1 if up else -1
        part = back_part(far, z + shift * (STEPS[channel] - step))
        if step:
            backs[channel, step - 1].wait_recv()
            part = part + back_in[channel, step - 1].astype(F32)
        back_out[channel, step] = part.astype(BF16)
        backs[channel, step] = send(
            back_out.at[channel, step], back_in.at[channel, step],
            back_send.at[channel, step], back_recv.at[channel, step],
            row, up_col if up else down_col,
        )

    for channel in (FAR_DOWN, OWN_UP, FAR_UP, OWN_DOWN):
        back_step(channel, 0)
    reduce.spread()
    for step in (1, 2, 3):
        for channel in (FAR_DOWN, OWN_UP, FAR_UP, OWN_DOWN):
            if step < STEPS[channel]:
                back_step(channel, step)

    def back_total(far):
        total = back_part(far, z)
        for channel in (FAR_UP, FAR_DOWN) if far else (OWN_UP, OWN_DOWN):
            step = STEPS[channel] - 1
            backs[channel, step].wait_recv()
            total = total + back_in[channel, step].astype(F32)
        return total

    mean = reduce.finish().reshape(nodes, px_ref.shape[2])
    back_far_out[...] = back_total(True).astype(BF16)
    back_far = send(
        back_far_out, back_far_in, back_far_sems.at[0], back_far_sems.at[1], row, far_col
    )
    mean_buf[...] = mean
    pre = wide_dot(mean, w1_ref[...])
    pre_buf[...] = pre
    hidden = pre * (1.0 / (1.0 + jnp.exp(-pre)))
    h_buf[...] = wide_dot(hidden, w2_ref[...]).astype(BF16)
    gather.start()
    own = pltpu.make_async_copy(h_buf, gh_ref.at[col], own_sem)
    own.start()

    back_own = back_total(False)
    gather.phase(0)
    back_far.wait_recv()
    back = back_own + back_far_in[...].astype(F32)
    back_high, back_low = halves(back)
    across = (((1,), (1,)), ((), ()))
    hidden_grad = lax.dot_general(
        back_high, w2_ref[...], across, preferred_element_type=F32
    ) + lax.dot_general(back_low, w2_ref[...], across, preferred_element_type=F32)
    pre = pre_buf[...]
    sigma = 1.0 / (1.0 + jnp.exp(-pre))
    pre_grad = hidden_grad * (sigma * (1.0 + pre * (1.0 - sigma)))
    contract = (((0,), (0,)), ((), ()))
    gather.phase(1)
    second = split_dot(pre * sigma, back, contract)
    first = split_dot(mean_buf[...], pre_grad, contract)
    wide = first.shape[0]
    grad_buf[0:wide] = first[:, :width] * scale
    grad_buf[wide : 2 * wide] = first[:, width:] * scale
    grad_buf[2 * wide : 3 * wide] = second * scale
    half = grad_buf.shape[0] // 2
    share = half // CHIPS
    pair = send(
        grad_buf.at[pl.ds((1 - core) * half, half)], grad_pair,
        pair_sems.at[0], pair_sems.at[1], reduce.sibling, col,
    )
    gather.phase(2)
    pair.wait_recv()
    half_buf[...] = grad_buf[pl.ds(core * half, half)] + grad_pair[...]
    grads = []
    for i, there in enumerate(reduce.rows):
        grads.append(
            send(
                half_buf.at[pl.ds(lax.div(there, 2) * share, share)], grad_in.at[i],
                grad_send.at[i], grad_recv.at[i], there, col,
            )
        )
    gather.phase(3)
    gather.phase(4)
    total = half_buf[pl.ds(lax.div(row, 2) * share, share)]
    for i, copy in enumerate(grads):
        copy.wait_recv()
        total = total + grad_in[i]
    share_ref[...] = total.astype(BF16)
    reduce.drain()
    gather.drain()
    for copy in list(backs.values()) + [back_far, pair] + grads:
        copy.wait_send()
    own.wait()


def middle(px, pb, w1, w2, scale):
    edge, wide = px.shape[1:]
    width = pb.shape[2]
    nodes = 2 * edge
    grad_rows = 3 * wide
    share = grad_rows // ROW
    return pl.pallas_call(
        functools.partial(middle_kernel, scale),
        out_shape=(
            jax.ShapeDtypeStruct((COL, nodes, width), BF16),
            jax.ShapeDtypeStruct((share, width), BF16),
        ),
        in_specs=[ANY, WHOLE, WHOLE, WHOLE],
        out_specs=(ANY, WHOLE),
        scratch_shapes=row_reduce_scratch(edge, wide)
        + [
            pltpu.VMEM((4, 4, nodes, width), BF16),
            pltpu.VMEM((4, 4, nodes, width), BF16),
            DMA((4, 4)), DMA((4, 4)),
            pltpu.VMEM((nodes, width), BF16),
            pltpu.VMEM((nodes, width), BF16),
            DMA((2,)),
            pltpu.VMEM((nodes, width), BF16),
            *gather_sems(2), DMA,
            pltpu.VMEM((nodes, wide), F32),
            pltpu.VMEM((nodes, wide), F32),
            pltpu.VMEM((grad_rows, width), F32),
            pltpu.VMEM((grad_rows // 2, width), F32),
            DMA((2,)),
            pltpu.VMEM((grad_rows // 2, width), F32),
            pltpu.VMEM((CHIPS - 1, share, width), F32),
            DMA((CHIPS - 1,)), DMA((CHIPS - 1,)),
        ],
        compiler_params=pltpu.CompilerParams(collective_id=1, has_side_effects=True, vmem_limit_bytes=SCOPED),
        name="middle",
    )(px, pb, w1, w2)


def last_kernel(
    ps_ref, share_ref,
    out_ref, grad_ref,
    held, pair_in, out_buf, in_buf, pair_send, pair_recv, near_send, near_recv, load_sems,
    col_in, col_send, col_recv, own_sem,
    sum_buf, row_send, row_recv, twin_send, twin_recv,
):
    row, col, core, x_lo, y, x_hi, z = where_am_i()
    reduce = RowReduce(
        ps_ref, held, pair_in, out_buf, in_buf, pair_send, pair_recv, near_send, near_recv, load_sems
    )
    cols = [lax.rem(col + k, COL) for k in range(1, COL)]
    sibling = reduce.sibling
    meet([(there, col) for there in [sibling] + reduce.rows] + [(row, there) for there in cols])
    across = []
    for k, there in enumerate(cols):
        across.append(
            send(share_ref, col_in.at[col], col_send.at[k], col_recv.at[k], row, there)
        )
    reduce.start()
    own = pltpu.make_async_copy(share_ref, col_in.at[col], own_sem)
    own.start()
    reduce.spread()
    own.wait()
    for copy in across:
        copy.wait_recv()
    total = col_in[0].astype(F32)
    for k in range(1, COL):
        total = total + col_in[k].astype(F32)
    sum_buf[...] = total
    share = share_ref.shape[0]

    def place(chip):
        return pl.ds((core * CHIPS + chip) * share, share)

    mine = place(lax.div(row, 2))
    grad_ref[mine] = total
    along = []
    for i, there in enumerate(reduce.rows):
        along.append(
            send(sum_buf, grad_ref.at[mine], row_send.at[i], row_recv.at[i], there, col)
        )
    twins = [send(sum_buf, grad_ref.at[mine], twin_send.at[7], twin_recv.at[7], sibling, col)]
    out_ref[...] = reduce.finish().reshape(out_ref.shape)
    for i, (dx, dy) in enumerate(NEAR):
        from_x = lax.rem(x_lo + dx, 2)
        from_y = lax.rem(y - dy + Y, Y)
        along[i].wait_recv()
        theirs = place(from_x * Y + from_y)
        twins.append(
            send(
                grad_ref.at[theirs], grad_ref.at[theirs],
                twin_send.at[i], twin_recv.at[i], sibling, col,
            )
        )
    for copy in twins:
        copy.wait_recv()
    reduce.drain()
    for copy in across + along + twins:
        copy.wait_send()


def last(ps, share):
    edge, width = ps.shape[1:]
    return pl.pallas_call(
        last_kernel,
        out_shape=(
            jax.ShapeDtypeStruct((2 * edge, width), F32),
            jax.ShapeDtypeStruct((ROW * share.shape[0], width), F32),
        ),
        in_specs=[ANY, WHOLE],
        out_specs=(WHOLE, WHOLE),
        scratch_shapes=row_reduce_scratch(edge, width)
        + [
            pltpu.VMEM((COL,) + share.shape, BF16),
            DMA((COL - 1,)), DMA((COL - 1,)), DMA,
            pltpu.VMEM(share.shape, F32),
            DMA((7,)), DMA((7,)), DMA((8,)), DMA((8,)),
        ],
        compiler_params=pltpu.CompilerParams(collective_id=2, has_side_effects=True, vmem_limit_bytes=SCOPED),
        name="last",
    )(ps, share)


def arrange_kernel(out_ref, grad_ref, output_ref, first_ref, second_ref):
    wide = first_ref.shape[0]
    width = second_ref.shape[1]
    output_ref[...] = out_ref[...].astype(BF16)
    first_ref[:, :width] = grad_ref[:wide]
    first_ref[:, width:] = grad_ref[wide : 2 * wide]
    second_ref[...] = grad_ref[2 * wide :]


def arrange(out, grads, wide):
    return pl.pallas_call(
        arrange_kernel,
        out_shape=(
            jax.ShapeDtypeStruct(out.shape, BF16),
            jax.ShapeDtypeStruct((wide, 2 * grads.shape[1]), F32),
            jax.ShapeDtypeStruct((wide, grads.shape[1]), F32),
        ),
        in_specs=[WHOLE, WHOLE],
        out_specs=(WHOLE, WHOLE, WHOLE),
        compiler_params=pltpu.CompilerParams(vmem_limit_bytes=SCOPED),
        name="arrange",
    )(out, grads)


def in_hbm(array):
    return pltpu.with_memory_space_constraint(array, pltpu.HBM)


def on_device(
    node_features, tile_values, tile_coords, tile_counts, first_weight, second_weight, out_grad
):
    edge = tile_values.shape[-1]
    slots = tile_values.shape[2]
    tiles = tile_values.reshape(slots, edge, edge)
    coords = in_hbm(tile_coords.reshape(slots, 2).T)
    count = tile_counts.reshape(1)
    scale = 1.0 / math.sqrt(node_features.shape[0] * ROW * COL)
    gx, gg, tiles = gather_inputs(in_hbm(node_features), in_hbm(out_grad), in_hbm(tiles))
    px, pb = propagate(
        both_kernel, coords, count, tiles,
        [gx.reshape(-1, edge, gx.shape[-1]), gg.reshape(-1, edge, gg.shape[-1])], "both",
    )
    gh, share = middle(px, pb, first_weight, second_weight, scale)
    (ps,) = propagate(
        one_kernel, coords, count, tiles, [gh.reshape(-1, edge, gh.shape[-1])], "one"
    )
    out, grads = last(ps, share)
    return arrange(out, grads, first_weight.shape[0])


def solution(mesh):
    return jax.shard_map(
        on_device,
        mesh=mesh,
        in_specs=(
            P(("row", "col"), None),
            P("row", "col", None, None, None),
            P("row", "col", None, None),
            P("row", "col"),
            P(),
            P(),
            P(("row", "col"), None),
        ),
        out_specs=(P(("row", "col"), None), P(), P()),
        check_vma=False,
    )
```

```python
import functools
import math

import jax
import jax.numpy as jnp
from jax import lax
from jax.experimental import pallas as pl
from jax.experimental.pallas import tpu as pltpu
from jax.sharding import PartitionSpec as P

MESH = pl.DeviceIdType.MESH
ANY = pl.BlockSpec(memory_space=pl.ANY)
WHOLE = pl.BlockSpec(memory_space=pltpu.VMEM)
DMA = pltpu.SemaphoreType.DMA
F32 = jnp.float32
BF16 = jnp.bfloat16

Y = 4
Z = 8
CHIPS = 8
ROW = 16
COL = 16
NEAR = ((1, 2), (1, 1), (1, 3), (0, 2), (0, 1), (0, 3), (1, 0))
OWN_UP, OWN_DOWN, FAR_UP, FAR_DOWN = 0, 1, 2, 3
STEPS = (4, 3, 3, 4)
TILES_AT_ONCE = 16
SCOPED = 24 * 2**20
GROUP = 4


def where_am_i():
    row = lax.axis_index("row")
    col = lax.axis_index("col")
    core = lax.rem(row, 2)
    chip = lax.div(row, 2)
    y = lax.rem(chip, Y)
    x_lo = lax.div(chip, Y)
    z = lax.rem(col, Z)
    x_hi = lax.div(col, Z)
    return row, col, core, x_lo, y, x_hi, z


def send(src, dst, send_sem, recv_sem, row, col):
    copy = pltpu.make_async_remote_copy(
        src_ref=src,
        dst_ref=dst,
        send_sem=send_sem,
        recv_sem=recv_sem,
        device_id=(row, col),
        device_id_type=MESH,
    )
    copy.start()
    return copy


def meet(partners):
    barrier = pltpu.get_barrier_semaphore()
    for partner in partners:
        pl.semaphore_signal(barrier, inc=1, device_id=partner, device_id_type=MESH)
    pl.semaphore_wait(barrier, len(partners))


def near_chips(x_lo, y, core):
    rows = []
    for dx, dy in NEAR:
        there_x = lax.rem(x_lo + dx, 2)
        there_y = lax.rem(y + dy, Y)
        rows.append((there_x * Y + there_y) * 2 + core)
    return rows


class ColGather:
    def __init__(self, mine, gathered, ring_send, ring_recv, far_send, far_recv):
        self.mine = mine
        self.gathered = gathered
        self.ring_send = ring_send
        self.ring_recv = ring_recv
        self.row, self.col, _, _, _, self.x_hi, self.z = where_am_i()
        self.far_send = far_send
        self.far_recv = far_recv
        self.pieces = far_send.shape[0]
        self.size = mine.shape[0] // self.pieces
        self.rings = {}
        self.exchange = []

    def block(self, far, z):
        x_hi = 1 - self.x_hi if far else self.x_hi
        return x_hi * Z + lax.rem(z + Z, Z)

    def ring(self, channel, step, piece):
        up = channel in (OWN_UP, FAR_UP)
        far = channel in (FAR_UP, FAR_DOWN)
        shift = 1 if up else -1
        slot = self.block(far, self.z - shift * step)
        rows = pl.ds(piece * self.size, self.size)
        there = self.gathered.at[slot, rows]
        self.rings[channel, step, piece] = send(
            self.mine.at[rows] if (step == 0 and not far) else there,
            there,
            self.ring_send.at[channel, step, piece],
            self.ring_recv.at[channel, step, piece],
            self.row,
            self.block(False, self.z + shift),
        )

    def start(self):
        for piece in range(self.pieces):
            rows = pl.ds(piece * self.size, self.size)
            self.exchange.append(
                send(
                    self.mine.at[rows],
                    self.gathered.at[self.col, rows],
                    self.far_send.at[piece],
                    self.far_recv.at[piece],
                    self.row,
                    self.block(True, self.z),
                )
            )
            self.ring(OWN_UP, 0, piece)
            self.ring(OWN_DOWN, 0, piece)

    def pass_on(self, channel, step, piece):
        if step <= STEPS[channel]:
            self.rings[channel, step - 1, piece].wait_recv()
        if step < STEPS[channel]:
            self.ring(channel, step, piece)

    def phase(self, number):
        for piece in range(self.pieces):
            self.pass_on(OWN_UP, number + 1, piece)
            self.pass_on(OWN_DOWN, number + 1, piece)
            if number == 0:
                self.exchange[piece].wait_recv()
                self.ring(FAR_UP, 0, piece)
                self.ring(FAR_DOWN, 0, piece)
            else:
                self.pass_on(FAR_UP, number, piece)
                self.pass_on(FAR_DOWN, number, piece)

    def drain(self):
        for copy in self.exchange + list(self.rings.values()):
            copy.wait_send()


PHASES = 5


def gather_sems(pieces):
    return [DMA((4, 4, pieces)), DMA((4, 4, pieces)), DMA((pieces,)), DMA((pieces,))]


def gather_kernel(
    x_ref, g_ref, tiles_ref, gx_ref, gg_ref, near_tiles_ref,
    ring_send, ring_recv, far_send, far_recv, near_send, near_recv, pair_send, pair_recv, own_sems,
):
    row, col, core, x_lo, y, x_hi, z = where_am_i()
    rows = near_chips(x_lo, y, core)
    sibling = row + 1 - 2 * core
    gather = ColGather(x_ref, gx_ref, ring_send, ring_recv, far_send, far_recv)
    meet(
        [(row, gather.block(False, z + 1)), (row, gather.block(False, z - 1)), (row, gather.block(True, z))]
        + [(there, col) for there in rows]
        + [(sibling, col)]
    )
    gather.start()
    own_x = pltpu.make_async_copy(x_ref, gx_ref.at[col], own_sems.at[0])
    own_x.start()
    own_g = pltpu.make_async_copy(g_ref, gg_ref.at[row], own_sems.at[1])
    own_g.start()
    to_pair = [send(g_ref, gg_ref.at[row], pair_send.at[7], pair_recv.at[7], sibling, col)]
    to_near = []
    for i, there in enumerate(rows):
        to_near.append(
            send(g_ref, gg_ref.at[row], near_send.at[i], near_recv.at[i], there, col)
        )
    own_tiles = pltpu.make_async_copy(tiles_ref, near_tiles_ref, own_sems.at[2])
    own_tiles.start()
    gather.phase(0)
    gather.phase(1)
    for i, (dx, dy) in enumerate(NEAR):
        from_x = lax.rem(x_lo + dx, 2)
        from_y = lax.rem(y - dy + Y, Y)
        origin = (from_x * Y + from_y) * 2 + core
        to_near[i].wait_recv()
        to_pair.append(
            send(gg_ref.at[origin], gg_ref.at[origin], pair_send.at[i], pair_recv.at[i], sibling, col)
        )
    for number in range(2, PHASES):
        gather.phase(number)
    gather.drain()
    for copy in to_pair:
        copy.wait_recv()
    for copy in to_pair + to_near:
        copy.wait_send()
    own_x.wait()
    own_g.wait()
    own_tiles.wait()


def gather_inputs(x, g, tiles):
    return pl.pallas_call(
        gather_kernel,
        out_shape=(
            jax.ShapeDtypeStruct((COL,) + x.shape, x.dtype),
            jax.ShapeDtypeStruct((ROW,) + g.shape, g.dtype),
            jax.ShapeDtypeStruct(tiles.shape, tiles.dtype),
        ),
        in_specs=[ANY, ANY, ANY],
        out_specs=(ANY, ANY, ANY),
        scratch_shapes=[
            *gather_sems(2),
            DMA((7,)), DMA((7,)), DMA((8,)), DMA((8,)), DMA((3,)),
        ],
        compiler_params=pltpu.CompilerParams(collective_id=0, has_side_effects=True, vmem_limit_bytes=SCOPED),
        name="gather_inputs",
    )(x, g, tiles)


def both_kernel(coords, count, tiles, xg, gg, px, pb):
    step = pl.program_id(0)
    dead_row = px.shape[0] - 1

    @pl.when(step == 0)
    def _():
        px[...] = jnp.zeros_like(px)
        pb[...] = jnp.zeros_like(pb)

    @pl.when(step * TILES_AT_ONCE < count[0])
    def _():
        for first in range(0, TILES_AT_ONCE, GROUP):
            places = []
            for j in range(first, first + GROUP):
                slot = step * TILES_AT_ONCE + j
                live = slot < count[0]
                r = coords[0, slot]
                c = coords[1, slot]
                tile = tiles[j]
                forward = jnp.dot(tile, xg[c], preferred_element_type=F32)
                back = lax.dot_general(
                    tile, gg[r], (((0,), (0,)), ((), ())), preferred_element_type=F32
                )
                places.append(
                    (jnp.where(live, r, dead_row), jnp.where(live, c, dead_row), forward, back)
                )
            for r, c, forward, back in places:
                px[r] += forward
                pb[c] += back


def one_kernel(coords, count, tiles, xg, px):
    step = pl.program_id(0)
    dead_row = px.shape[0] - 1

    @pl.when(step == 0)
    def _():
        px[...] = jnp.zeros_like(px)

    @pl.when(step * TILES_AT_ONCE < count[0])
    def _():
        for first in range(0, TILES_AT_ONCE, GROUP):
            places = []
            for j in range(first, first + GROUP):
                slot = step * TILES_AT_ONCE + j
                live = slot < count[0]
                r = coords[0, slot]
                c = coords[1, slot]
                forward = jnp.dot(tiles[j], xg[c], preferred_element_type=F32)
                places.append((jnp.where(live, r, dead_row), forward))
            for r, forward in places:
                px[r] += forward


def propagate(kernel, coords, count, tiles, sources, name):
    slots, edge, _ = tiles.shape
    whole = lambda shape: pl.BlockSpec(shape, lambda i, *_: (0, 0, 0))
    outs = []
    for source in sources:
        outs.append((source.shape[0] + 1,) + source.shape[1:])
    return pl.pallas_call(
        kernel,
        out_shape=tuple(jax.ShapeDtypeStruct(out, F32) for out in outs),
        grid_spec=pltpu.PrefetchScalarGridSpec(
            num_scalar_prefetch=2,
            grid=(slots // TILES_AT_ONCE,),
            in_specs=[pl.BlockSpec((TILES_AT_ONCE, edge, edge), lambda i, *_: (i, 0, 0))]
            + [whole(source.shape) for source in sources],
            out_specs=tuple(whole(out) for out in outs),
        ),
        compiler_params=pltpu.CompilerParams(vmem_limit_bytes=SCOPED),
        name=name,
    )(coords, count, tiles, *sources)


def halves(value):
    high = value.astype(BF16)
    return high, (value - high.astype(F32)).astype(BF16)


def wide_dot(value, weight):
    high, low = halves(value)
    return jnp.dot(high, weight, preferred_element_type=F32) + jnp.dot(
        low, weight, preferred_element_type=F32
    )


def split_dot(left, right, contract):
    left_high, left_low = halves(left)
    right_high, right_low = halves(right)
    total = lax.dot_general(left_high, right_high, contract, preferred_element_type=F32)
    total += lax.dot_general(left_high, right_low, contract, preferred_element_type=F32)
    total += lax.dot_general(left_low, right_high, contract, preferred_element_type=F32)
    return total


class RowReduce:
    def __init__(self, parts, held, pair_in, out_buf, in_buf, pair_send, pair_recv, near_send, near_recv, load_sems):
        self.row, self.col, self.core, self.x_lo, self.y, _, _ = where_am_i()
        self.parts, self.held, self.pair_in = parts, held, pair_in
        self.out_buf, self.in_buf = out_buf, in_buf
        self.pair_send, self.pair_recv = pair_send, pair_recv
        self.near_send, self.near_recv = near_send, near_recv
        self.load_sems = load_sems
        self.sibling = self.row + 1 - 2 * self.core
        self.rows = near_chips(self.x_lo, self.y, self.core)

    def start(self):
        self.pairs, self.loads = [], []
        for i, there in enumerate(self.rows + [self.row]):
            other = there + 1 - 2 * self.core
            self.pairs.append(
                send(
                    self.parts.at[pl.ds(2 * other, 2)], self.pair_in.at[i],
                    self.pair_send.at[i], self.pair_recv.at[i], self.sibling, self.col,
                )
            )
            load = pltpu.make_async_copy(
                self.parts.at[pl.ds(2 * there, 2)], self.held.at[i], self.load_sems.at[i]
            )
            load.start()
            self.loads.append(load)

    def spread(self):
        self.nears = []
        for i, there in enumerate(self.rows):
            self.pairs[i].wait_recv()
            self.loads[i].wait()
            self.out_buf[i] = (self.pair_in[i] + self.held[i]).astype(BF16)
            self.nears.append(
                send(
                    self.out_buf.at[i], self.in_buf.at[i],
                    self.near_send.at[i], self.near_recv.at[i], there, self.col,
                )
            )

    def finish(self):
        self.pairs[7].wait_recv()
        self.loads[7].wait()
        total = self.pair_in[7] + self.held[7]
        for i in range(7):
            self.nears[i].wait_recv()
            total = total + self.in_buf[i].astype(F32)
        return total

    def drain(self):
        for copy in self.pairs + self.nears:
            copy.wait_send()


def row_reduce_scratch(edge, width):
    return [
        pltpu.VMEM((8, 2, edge, width), F32),
        pltpu.VMEM((8, 2, edge, width), F32),
        pltpu.VMEM((7, 2, edge, width), BF16),
        pltpu.VMEM((7, 2, edge, width), BF16),
        DMA((8,)), DMA((8,)), DMA((7,)), DMA((7,)), DMA((8,)),
    ]


def middle_kernel(
    scale,
    px_ref, pb_ref, w1_ref, w2_ref,
    gh_ref, share_ref,
    held, pair_in, out_buf, in_buf, pair_send, pair_recv, near_send, near_recv, load_sems,
    back_out, back_in, back_send, back_recv, back_far_out, back_far_in, back_far_sems,
    h_buf, ring_send, ring_recv, far_send, far_recv, own_sem,
    mean_buf, pre_buf, grad_buf, grad_pair, pair_sems, half_buf, grad_in, grad_send, grad_recv,
):
    row, col, core, x_lo, y, x_hi, z = where_am_i()
    reduce = RowReduce(
        px_ref, held, pair_in, out_buf, in_buf, pair_send, pair_recv, near_send, near_recv, load_sems
    )
    gather = ColGather(h_buf, gh_ref, ring_send, ring_recv, far_send, far_recv)
    far_col = gather.block(True, z)
    up_col = gather.block(False, z + 1)
    down_col = gather.block(False, z - 1)
    partners = [(there, col) for there in [reduce.sibling] + reduce.rows]
    meet([(row, up_col), (row, down_col), (row, far_col)] + partners)
    reduce.start()

    nodes = 2 * pb_ref.shape[1]
    width = pb_ref.shape[2]

    def back_part(far, z_to):
        block = gather.block(far, z_to)
        return pb_ref[pl.ds(2 * block, 2)].reshape(nodes, width)

    backs = {}

    def back_step(channel, step):
        up = channel in (OWN_UP, FAR_UP)
        far = channel in (FAR_UP, FAR_DOWN)
        shift = 1 if up else -1
        part = back_part(far, z + shift * (STEPS[channel] - step))
        if step:
            backs[channel, step - 1].wait_recv()
            part = part + back_in[channel, step - 1].astype(F32)
        back_out[channel, step] = part.astype(BF16)
        backs[channel, step] = send(
            back_out.at[channel, step], back_in.at[channel, step],
            back_send.at[channel, step], back_recv.at[channel, step],
            row, up_col if up else down_col,
        )

    for channel in (FAR_DOWN, OWN_UP, FAR_UP, OWN_DOWN):
        back_step(channel, 0)
    reduce.spread()
    for step in (1, 2, 3):
        for channel in (FAR_DOWN, OWN_UP, FAR_UP, OWN_DOWN):
            if step < STEPS[channel]:
                back_step(channel, step)

    def back_total(far):
        total = back_part(far, z)
        for channel in (FAR_UP, FAR_DOWN) if far else (OWN_UP, OWN_DOWN):
            step = STEPS[channel] - 1
            backs[channel, step].wait_recv()
            total = total + back_in[channel, step].astype(F32)
        return total

    mean = reduce.finish().reshape(nodes, px_ref.shape[2])
    back_far_out[...] = back_total(True).astype(BF16)
    back_far = send(
        back_far_out, back_far_in, back_far_sems.at[0], back_far_sems.at[1], row, far_col
    )
    mean_buf[...] = mean
    pre = wide_dot(mean, w1_ref[...])
    pre_buf[...] = pre
    hidden = pre * (1.0 / (1.0 + jnp.exp(-pre)))
    h_buf[...] = wide_dot(hidden, w2_ref[...]).astype(BF16)
    gather.start()
    own = pltpu.make_async_copy(h_buf, gh_ref.at[col], own_sem)
    own.start()

    back_own = back_total(False)
    gather.phase(0)
    back_far.wait_recv()
    back = back_own + back_far_in[...].astype(F32)
    back_high, back_low = halves(back)
    across = (((1,), (1,)), ((), ()))
    hidden_grad = lax.dot_general(
        back_high, w2_ref[...], across, preferred_element_type=F32
    ) + lax.dot_general(back_low, w2_ref[...], across, preferred_element_type=F32)
    pre = pre_buf[...]
    sigma = 1.0 / (1.0 + jnp.exp(-pre))
    pre_grad = hidden_grad * (sigma * (1.0 + pre * (1.0 - sigma)))
    contract = (((0,), (0,)), ((), ()))
    gather.phase(1)
    second = split_dot(pre * sigma, back, contract)
    first = split_dot(mean_buf[...], pre_grad, contract)
    wide = first.shape[0]
    grad_buf[0:wide] = first[:, :width] * scale
    grad_buf[wide : 2 * wide] = first[:, width:] * scale
    grad_buf[2 * wide : 3 * wide] = second * scale
    half = grad_buf.shape[0] // 2
    share = half // CHIPS
    pair = send(
        grad_buf.at[pl.ds((1 - core) * half, half)], grad_pair,
        pair_sems.at[0], pair_sems.at[1], reduce.sibling, col,
    )
    gather.phase(2)
    pair.wait_recv()
    half_buf[...] = grad_buf[pl.ds(core * half, half)] + grad_pair[...]
    grads = []
    for i, there in enumerate(reduce.rows):
        grads.append(
            send(
                half_buf.at[pl.ds(lax.div(there, 2) * share, share)], grad_in.at[i],
                grad_send.at[i], grad_recv.at[i], there, col,
            )
        )
    gather.phase(3)
    gather.phase(4)
    total = half_buf[pl.ds(lax.div(row, 2) * share, share)]
    for i, copy in enumerate(grads):
        copy.wait_recv()
        total = total + grad_in[i]
    share_ref[...] = total.astype(BF16)
    reduce.drain()
    gather.drain()
    for copy in list(backs.values()) + [back_far, pair] + grads:
        copy.wait_send()
    own.wait()


def middle(px, pb, w1, w2, scale):
    edge, wide = px.shape[1:]
    width = pb.shape[2]
    nodes = 2 * edge
    grad_rows = 3 * wide
    share = grad_rows // ROW
    return pl.pallas_call(
        functools.partial(middle_kernel, scale),
        out_shape=(
            jax.ShapeDtypeStruct((COL, nodes, width), BF16),
            jax.ShapeDtypeStruct((share, width), BF16),
        ),
        in_specs=[ANY, WHOLE, WHOLE, WHOLE],
        out_specs=(ANY, WHOLE),
        scratch_shapes=row_reduce_scratch(edge, wide)
        + [
            pltpu.VMEM((4, 4, nodes, width), BF16),
            pltpu.VMEM((4, 4, nodes, width), BF16),
            DMA((4, 4)), DMA((4, 4)),
            pltpu.VMEM((nodes, width), BF16),
            pltpu.VMEM((nodes, width), BF16),
            DMA((2,)),
            pltpu.VMEM((nodes, width), BF16),
            *gather_sems(2), DMA,
            pltpu.VMEM((nodes, wide), F32),
            pltpu.VMEM((nodes, wide), F32),
            pltpu.VMEM((grad_rows, width), F32),
            pltpu.VMEM((grad_rows // 2, width), F32),
            DMA((2,)),
            pltpu.VMEM((grad_rows // 2, width), F32),
            pltpu.VMEM((CHIPS - 1, share, width), F32),
            DMA((CHIPS - 1,)), DMA((CHIPS - 1,)),
        ],
        compiler_params=pltpu.CompilerParams(collective_id=1, has_side_effects=True, vmem_limit_bytes=SCOPED),
        name="middle",
    )(px, pb, w1, w2)


def last_kernel(
    ps_ref, share_ref,
    out_ref, grad_ref,
    held, pair_in, out_buf, in_buf, pair_send, pair_recv, near_send, near_recv, load_sems,
    col_in, col_send, col_recv, own_sem,
    sum_buf, row_send, row_recv, twin_send, twin_recv,
):
    row, col, core, x_lo, y, x_hi, z = where_am_i()
    reduce = RowReduce(
        ps_ref, held, pair_in, out_buf, in_buf, pair_send, pair_recv, near_send, near_recv, load_sems
    )
    cols = [lax.rem(col + k, COL) for k in range(1, COL)]
    sibling = reduce.sibling
    meet([(there, col) for there in [sibling] + reduce.rows] + [(row, there) for there in cols])
    across = []
    for k, there in enumerate(cols):
        across.append(
            send(share_ref, col_in.at[col], col_send.at[k], col_recv.at[k], row, there)
        )
    reduce.start()
    own = pltpu.make_async_copy(share_ref, col_in.at[col], own_sem)
    own.start()
    reduce.spread()
    own.wait()
    for copy in across:
        copy.wait_recv()
    total = col_in[0].astype(F32)
    for k in range(1, COL):
        total = total + col_in[k].astype(F32)
    sum_buf[...] = total
    share = share_ref.shape[0]

    def place(chip):
        return pl.ds((core * CHIPS + chip) * share, share)

    mine = place(lax.div(row, 2))
    grad_ref[mine] = total
    along = []
    for i, there in enumerate(reduce.rows):
        along.append(
            send(sum_buf, grad_ref.at[mine], row_send.at[i], row_recv.at[i], there, col)
        )
    twins = [send(sum_buf, grad_ref.at[mine], twin_send.at[7], twin_recv.at[7], sibling, col)]
    out_ref[...] = reduce.finish().reshape(out_ref.shape)
    for i, (dx, dy) in enumerate(NEAR):
        from_x = lax.rem(x_lo + dx, 2)
        from_y = lax.rem(y - dy + Y, Y)
        along[i].wait_recv()
        theirs = place(from_x * Y + from_y)
        twins.append(
            send(
                grad_ref.at[theirs], grad_ref.at[theirs],
                twin_send.at[i], twin_recv.at[i], sibling, col,
            )
        )
    for copy in twins:
        copy.wait_recv()
    reduce.drain()
    for copy in across + along + twins:
        copy.wait_send()


def last(ps, share):
    edge, width = ps.shape[1:]
    return pl.pallas_call(
        last_kernel,
        out_shape=(
            jax.ShapeDtypeStruct((2 * edge, width), F32),
            jax.ShapeDtypeStruct((ROW * share.shape[0], width), F32),
        ),
        in_specs=[ANY, WHOLE],
        out_specs=(WHOLE, WHOLE),
        scratch_shapes=row_reduce_scratch(edge, width)
        + [
            pltpu.VMEM((COL,) + share.shape, BF16),
            DMA((COL - 1,)), DMA((COL - 1,)), DMA,
            pltpu.VMEM(share.shape, F32),
            DMA((7,)), DMA((7,)), DMA((8,)), DMA((8,)),
        ],
        compiler_params=pltpu.CompilerParams(collective_id=2, has_side_effects=True, vmem_limit_bytes=SCOPED),
        name="last",
    )(ps, share)


def arrange_kernel(out_ref, grad_ref, output_ref, first_ref, second_ref):
    wide = first_ref.shape[0]
    width = second_ref.shape[1]
    output_ref[...] = out_ref[...].astype(BF16)
    first_ref[:, :width] = grad_ref[:wide]
    first_ref[:, width:] = grad_ref[wide : 2 * wide]
    second_ref[...] = grad_ref[2 * wide :]


def arrange(out, grads, wide):
    return pl.pallas_call(
        arrange_kernel,
        out_shape=(
            jax.ShapeDtypeStruct(out.shape, BF16),
            jax.ShapeDtypeStruct((wide, 2 * grads.shape[1]), F32),
            jax.ShapeDtypeStruct((wide, grads.shape[1]), F32),
        ),
        in_specs=[WHOLE, WHOLE],
        out_specs=(WHOLE, WHOLE, WHOLE),
        compiler_params=pltpu.CompilerParams(vmem_limit_bytes=SCOPED),
        name="arrange",
    )(out, grads)


def in_hbm(array):
    return pltpu.with_memory_space_constraint(array, pltpu.HBM)


def on_device(
    node_features, tile_values, tile_coords, tile_counts, first_weight, second_weight, out_grad
):
    edge = tile_values.shape[-1]
    slots = tile_values.shape[2]
    tiles = tile_values.reshape(slots, edge, edge)
    coords = in_hbm(tile_coords.reshape(slots, 2).T)
    count = tile_counts.reshape(1)
    scale = 1.0 / math.sqrt(node_features.shape[0] * ROW * COL)
    gx, gg, tiles = gather_inputs(in_hbm(node_features), in_hbm(out_grad), in_hbm(tiles))
    px, pb = propagate(
        both_kernel, coords, count, tiles,
        [gx.reshape(-1, edge, gx.shape[-1]), gg.reshape(-1, edge, gg.shape[-1])], "both",
    )
    gh, share = middle(px, pb, first_weight, second_weight, scale)
    (ps,) = propagate(
        one_kernel, coords, count, tiles, [gh.reshape(-1, edge, gh.shape[-1])], "one"
    )
    out, grads = last(ps, share)
    return arrange(out, grads, first_weight.shape[0])


def solution(mesh):
    return jax.shard_map(
        on_device,
        mesh=mesh,
        in_specs=(
            P(("row", "col"), None),
            P("row", "col", None, None, None),
            P("row", "col", None, None),
            P("row", "col"),
            P(),
            P(),
            P(("row", "col"), None),
        ),
        out_specs=(P(("row", "col"), None), P(), P()),
        check_vma=False,
    )
```

```python
import functools
import math

import jax
import jax.numpy as jnp
from jax import lax
from jax.experimental import pallas as pl
from jax.experimental.pallas import tpu as pltpu
from jax.sharding import PartitionSpec as P

MESH = pl.DeviceIdType.MESH
ANY = pl.BlockSpec(memory_space=pl.ANY)
WHOLE = pl.BlockSpec(memory_space=pltpu.VMEM)
DMA = pltpu.SemaphoreType.DMA
F32 = jnp.float32
BF16 = jnp.bfloat16

Y = 4
Z = 8
CHIPS = 8
ROW = 16
COL = 16
NEAR = ((1, 2), (1, 1), (1, 3), (0, 2), (0, 1), (0, 3), (1, 0))
OWN_UP, OWN_DOWN, FAR_UP, FAR_DOWN = 0, 1, 2, 3
STEPS = (4, 3, 3, 4)
TILES_AT_ONCE = 16
SCOPED = 24 * 2**20
GROUP = 4


def where_am_i():
    row = lax.axis_index("row")
    col = lax.axis_index("col")
    core = lax.rem(row, 2)
    chip = lax.div(row, 2)
    y = lax.rem(chip, Y)
    x_lo = lax.div(chip, Y)
    z = lax.rem(col, Z)
    x_hi = lax.div(col, Z)
    return row, col, core, x_lo, y, x_hi, z


def send(src, dst, send_sem, recv_sem, row, col):
    copy = pltpu.make_async_remote_copy(
        src_ref=src,
        dst_ref=dst,
        send_sem=send_sem,
        recv_sem=recv_sem,
        device_id=(row, col),
        device_id_type=MESH,
    )
    copy.start()
    return copy


def meet(partners):
    barrier = pltpu.get_barrier_semaphore()
    for partner in partners:
        pl.semaphore_signal(barrier, inc=1, device_id=partner, device_id_type=MESH)
    pl.semaphore_wait(barrier, len(partners))


def near_chips(x_lo, y, core):
    rows = []
    for dx, dy in NEAR:
        there_x = lax.rem(x_lo + dx, 2)
        there_y = lax.rem(y + dy, Y)
        rows.append((there_x * Y + there_y) * 2 + core)
    return rows


class ColGather:
    def __init__(self, mine, gathered, ring_send, ring_recv, far_send, far_recv):
        self.mine = mine
        self.gathered = gathered
        self.ring_send = ring_send
        self.ring_recv = ring_recv
        self.row, self.col, _, _, _, self.x_hi, self.z = where_am_i()
        self.far_send = far_send
        self.far_recv = far_recv
        self.pieces = far_send.shape[0]
        self.size = mine.shape[0] // self.pieces
        self.rings = {}
        self.exchange = []

    def block(self, far, z):
        x_hi = 1 - self.x_hi if far else self.x_hi
        return x_hi * Z + lax.rem(z + Z, Z)

    def ring(self, channel, step, piece):
        up = channel in (OWN_UP, FAR_UP)
        far = channel in (FAR_UP, FAR_DOWN)
        shift = 1 if up else -1
        slot = self.block(far, self.z - shift * step)
        rows = pl.ds(piece * self.size, self.size)
        there = self.gathered.at[slot, rows]
        self.rings[channel, step, piece] = send(
            self.mine.at[rows] if (step == 0 and not far) else there,
            there,
            self.ring_send.at[channel, step, piece],
            self.ring_recv.at[channel, step, piece],
            self.row,
            self.block(False, self.z + shift),
        )

    def start(self):
        for piece in range(self.pieces):
            rows = pl.ds(piece * self.size, self.size)
            self.exchange.append(
                send(
                    self.mine.at[rows],
                    self.gathered.at[self.col, rows],
                    self.far_send.at[piece],
                    self.far_recv.at[piece],
                    self.row,
                    self.block(True, self.z),
                )
            )
            self.ring(OWN_UP, 0, piece)
            self.ring(OWN_DOWN, 0, piece)

    def pass_on(self, channel, step, piece):
        if step <= STEPS[channel]:
            self.rings[channel, step - 1, piece].wait_recv()
        if step < STEPS[channel]:
            self.ring(channel, step, piece)

    def phase(self, number):
        for piece in range(self.pieces):
            self.pass_on(OWN_UP, number + 1, piece)
            self.pass_on(OWN_DOWN, number + 1, piece)
            if number == 0:
                self.exchange[piece].wait_recv()
                self.ring(FAR_UP, 0, piece)
                self.ring(FAR_DOWN, 0, piece)
            else:
                self.pass_on(FAR_UP, number, piece)
                self.pass_on(FAR_DOWN, number, piece)

    def drain(self):
        for copy in self.exchange + list(self.rings.values()):
            copy.wait_send()


PHASES = 5


def gather_sems(pieces):
    return [DMA((4, 4, pieces)), DMA((4, 4, pieces)), DMA((pieces,)), DMA((pieces,))]


def gather_kernel(
    x_ref, g_ref, tiles_ref, gx_ref, gg_ref, near_tiles_ref,
    ring_send, ring_recv, far_send, far_recv, near_send, near_recv, pair_send, pair_recv, own_sems,
):
    row, col, core, x_lo, y, x_hi, z = where_am_i()
    rows = near_chips(x_lo, y, core)
    sibling = row + 1 - 2 * core
    gather = ColGather(x_ref, gx_ref, ring_send, ring_recv, far_send, far_recv)
    meet(
        [(row, gather.block(False, z + 1)), (row, gather.block(False, z - 1)), (row, gather.block(True, z))]
        + [(there, col) for there in rows]
        + [(sibling, col)]
    )
    gather.start()
    own_x = pltpu.make_async_copy(x_ref, gx_ref.at[col], own_sems.at[0])
    own_x.start()
    own_g = pltpu.make_async_copy(g_ref, gg_ref.at[row], own_sems.at[1])
    own_g.start()
    to_pair = [send(g_ref, gg_ref.at[row], pair_send.at[7], pair_recv.at[7], sibling, col)]
    to_near = []
    for i, there in enumerate(rows):
        to_near.append(
            send(g_ref, gg_ref.at[row], near_send.at[i], near_recv.at[i], there, col)
        )
    own_tiles = pltpu.make_async_copy(tiles_ref, near_tiles_ref, own_sems.at[2])
    own_tiles.start()
    gather.phase(0)
    gather.phase(1)
    for i, (dx, dy) in enumerate(NEAR):
        from_x = lax.rem(x_lo + dx, 2)
        from_y = lax.rem(y - dy + Y, Y)
        origin = (from_x * Y + from_y) * 2 + core
        to_near[i].wait_recv()
        to_pair.append(
            send(gg_ref.at[origin], gg_ref.at[origin], pair_send.at[i], pair_recv.at[i], sibling, col)
        )
    for number in range(2, PHASES):
        gather.phase(number)
    gather.drain()
    for copy in to_pair:
        copy.wait_recv()
    for copy in to_pair + to_near:
        copy.wait_send()
    own_x.wait()
    own_g.wait()
    own_tiles.wait()


def gather_inputs(x, g, tiles):
    return pl.pallas_call(
        gather_kernel,
        out_shape=(
            jax.ShapeDtypeStruct((COL,) + x.shape, x.dtype),
            jax.ShapeDtypeStruct((ROW,) + g.shape, g.dtype),
            jax.ShapeDtypeStruct(tiles.shape, tiles.dtype),
        ),
        in_specs=[ANY, ANY, ANY],
        out_specs=(ANY, ANY, ANY),
        scratch_shapes=[
            *gather_sems(4),
            DMA((7,)), DMA((7,)), DMA((8,)), DMA((8,)), DMA((3,)),
        ],
        compiler_params=pltpu.CompilerParams(collective_id=0, has_side_effects=True, vmem_limit_bytes=SCOPED),
        name="gather_inputs",
    )(x, g, tiles)


def both_kernel(coords, count, tiles, xg, gg, px, pb):
    step = pl.program_id(0)
    dead_row = px.shape[0] - 1

    @pl.when(step == 0)
    def _():
        px[...] = jnp.zeros_like(px)
        pb[...] = jnp.zeros_like(pb)

    @pl.when(step * TILES_AT_ONCE < count[0])
    def _():
        for first in range(0, TILES_AT_ONCE, GROUP):
            places = []
            for j in range(first, first + GROUP):
                slot = step * TILES_AT_ONCE + j
                live = slot < count[0]
                r = coords[0, slot]
                c = coords[1, slot]
                tile = tiles[j]
                forward = jnp.dot(tile, xg[c], preferred_element_type=F32)
                back = lax.dot_general(
                    tile, gg[r], (((0,), (0,)), ((), ())), preferred_element_type=F32
                )
                places.append(
                    (jnp.where(live, r, dead_row), jnp.where(live, c, dead_row), forward, back)
                )
            for r, c, forward, back in places:
                px[r] += forward
                pb[c] += back


def one_kernel(coords, count, tiles, xg, px):
    step = pl.program_id(0)
    dead_row = px.shape[0] - 1

    @pl.when(step == 0)
    def _():
        px[...] = jnp.zeros_like(px)

    @pl.when(step * TILES_AT_ONCE < count[0])
    def _():
        for first in range(0, TILES_AT_ONCE, GROUP):
            places = []
            for j in range(first, first + GROUP):
                slot = step * TILES_AT_ONCE + j
                live = slot < count[0]
                r = coords[0, slot]
                c = coords[1, slot]
                forward = jnp.dot(tiles[j], xg[c], preferred_element_type=F32)
                places.append((jnp.where(live, r, dead_row), forward))
            for r, forward in places:
                px[r] += forward


def propagate(kernel, coords, count, tiles, sources, name):
    slots, edge, _ = tiles.shape
    whole = lambda shape: pl.BlockSpec(shape, lambda i, *_: (0, 0, 0))
    outs = []
    for source in sources:
        outs.append((source.shape[0] + 1,) + source.shape[1:])
    return pl.pallas_call(
        kernel,
        out_shape=tuple(jax.ShapeDtypeStruct(out, F32) for out in outs),
        grid_spec=pltpu.PrefetchScalarGridSpec(
            num_scalar_prefetch=2,
            grid=(slots // TILES_AT_ONCE,),
            in_specs=[pl.BlockSpec((TILES_AT_ONCE, edge, edge), lambda i, *_: (i, 0, 0))]
            + [whole(source.shape) for source in sources],
            out_specs=tuple(whole(out) for out in outs),
        ),
        compiler_params=pltpu.CompilerParams(vmem_limit_bytes=SCOPED),
        name=name,
    )(coords, count, tiles, *sources)


def halves(value):
    high = value.astype(BF16)
    return high, (value - high.astype(F32)).astype(BF16)


def wide_dot(value, weight):
    high, low = halves(value)
    return jnp.dot(high, weight, preferred_element_type=F32) + jnp.dot(
        low, weight, preferred_element_type=F32
    )


def split_dot(left, right, contract):
    left_high, left_low = halves(left)
    right_high, right_low = halves(right)
    total = lax.dot_general(left_high, right_high, contract, preferred_element_type=F32)
    total += lax.dot_general(left_high, right_low, contract, preferred_element_type=F32)
    total += lax.dot_general(left_low, right_high, contract, preferred_element_type=F32)
    return total


class RowReduce:
    def __init__(self, parts, held, pair_in, out_buf, in_buf, pair_send, pair_recv, near_send, near_recv, load_sems):
        self.row, self.col, self.core, self.x_lo, self.y, _, _ = where_am_i()
        self.parts, self.held, self.pair_in = parts, held, pair_in
        self.out_buf, self.in_buf = out_buf, in_buf
        self.pair_send, self.pair_recv = pair_send, pair_recv
        self.near_send, self.near_recv = near_send, near_recv
        self.load_sems = load_sems
        self.sibling = self.row + 1 - 2 * self.core
        self.rows = near_chips(self.x_lo, self.y, self.core)

    def start(self):
        self.pairs, self.loads = [], []
        for i, there in enumerate(self.rows + [self.row]):
            other = there + 1 - 2 * self.core
            self.pairs.append(
                send(
                    self.parts.at[pl.ds(2 * other, 2)], self.pair_in.at[i],
                    self.pair_send.at[i], self.pair_recv.at[i], self.sibling, self.col,
                )
            )
            load = pltpu.make_async_copy(
                self.parts.at[pl.ds(2 * there, 2)], self.held.at[i], self.load_sems.at[i]
            )
            load.start()
            self.loads.append(load)

    def spread(self):
        self.nears = []
        for i, there in enumerate(self.rows):
            self.pairs[i].wait_recv()
            self.loads[i].wait()
            self.out_buf[i] = (self.pair_in[i] + self.held[i]).astype(BF16)
            self.nears.append(
                send(
                    self.out_buf.at[i], self.in_buf.at[i],
                    self.near_send.at[i], self.near_recv.at[i], there, self.col,
                )
            )

    def finish(self):
        self.pairs[7].wait_recv()
        self.loads[7].wait()
        total = self.pair_in[7] + self.held[7]
        for i in range(7):
            self.nears[i].wait_recv()
            total = total + self.in_buf[i].astype(F32)
        return total

    def drain(self):
        for copy in self.pairs + self.nears:
            copy.wait_send()


def row_reduce_scratch(edge, width):
    return [
        pltpu.VMEM((8, 2, edge, width), F32),
        pltpu.VMEM((8, 2, edge, width), F32),
        pltpu.VMEM((7, 2, edge, width), BF16),
        pltpu.VMEM((7, 2, edge, width), BF16),
        DMA((8,)), DMA((8,)), DMA((7,)), DMA((7,)), DMA((8,)),
    ]


def middle_kernel(
    scale,
    px_ref, pb_ref, w1_ref, w2_ref,
    gh_ref, share_ref,
    held, pair_in, out_buf, in_buf, pair_send, pair_recv, near_send, near_recv, load_sems,
    back_out, back_in, back_send, back_recv, back_far_out, back_far_in, back_far_sems,
    h_buf, ring_send, ring_recv, far_send, far_recv, own_sem,
    mean_buf, pre_buf, grad_buf, grad_pair, pair_sems, half_buf, grad_in, grad_send, grad_recv,
):
    row, col, core, x_lo, y, x_hi, z = where_am_i()
    reduce = RowReduce(
        px_ref, held, pair_in, out_buf, in_buf, pair_send, pair_recv, near_send, near_recv, load_sems
    )
    gather = ColGather(h_buf, gh_ref, ring_send, ring_recv, far_send, far_recv)
    far_col = gather.block(True, z)
    up_col = gather.block(False, z + 1)
    down_col = gather.block(False, z - 1)
    partners = [(there, col) for there in [reduce.sibling] + reduce.rows]
    meet([(row, up_col), (row, down_col), (row, far_col)] + partners)
    reduce.start()

    nodes = 2 * pb_ref.shape[1]
    width = pb_ref.shape[2]

    def back_part(far, z_to):
        block = gather.block(far, z_to)
        return pb_ref[pl.ds(2 * block, 2)].reshape(nodes, width)

    backs = {}

    def back_step(channel, step):
        up = channel in (OWN_UP, FAR_UP)
        far = channel in (FAR_UP, FAR_DOWN)
        shift = 1 if up else -1
        part = back_part(far, z + shift * (STEPS[channel] - step))
        if step:
            backs[channel, step - 1].wait_recv()
            part = part + back_in[channel, step - 1].astype(F32)
        back_out[channel, step] = part.astype(BF16)
        backs[channel, step] = send(
            back_out.at[channel, step], back_in.at[channel, step],
            back_send.at[channel, step], back_recv.at[channel, step],
            row, up_col if up else down_col,
        )

    for channel in (FAR_DOWN, OWN_UP, FAR_UP, OWN_DOWN):
        back_step(channel, 0)
    reduce.spread()
    for step in (1, 2, 3):
        for channel in (FAR_DOWN, OWN_UP, FAR_UP, OWN_DOWN):
            if step < STEPS[channel]:
                back_step(channel, step)

    def back_total(far):
        total = back_part(far, z)
        for channel in (FAR_UP, FAR_DOWN) if far else (OWN_UP, OWN_DOWN):
            step = STEPS[channel] - 1
            backs[channel, step].wait_recv()
            total = total + back_in[channel, step].astype(F32)
        return total

    mean = reduce.finish().reshape(nodes, px_ref.shape[2])
    back_far_out[...] = back_total(True).astype(BF16)
    back_far = send(
        back_far_out, back_far_in, back_far_sems.at[0], back_far_sems.at[1], row, far_col
    )
    mean_buf[...] = mean
    pre = wide_dot(mean, w1_ref[...])
    pre_buf[...] = pre
    hidden = pre * (1.0 / (1.0 + jnp.exp(-pre)))
    h_buf[...] = wide_dot(hidden, w2_ref[...]).astype(BF16)
    gather.start()
    own = pltpu.make_async_copy(h_buf, gh_ref.at[col], own_sem)
    own.start()

    back_own = back_total(False)
    gather.phase(0)
    back_far.wait_recv()
    back = back_own + back_far_in[...].astype(F32)
    back_high, back_low = halves(back)
    across = (((1,), (1,)), ((), ()))
    hidden_grad = lax.dot_general(
        back_high, w2_ref[...], across, preferred_element_type=F32
    ) + lax.dot_general(back_low, w2_ref[...], across, preferred_element_type=F32)
    pre = pre_buf[...]
    sigma = 1.0 / (1.0 + jnp.exp(-pre))
    pre_grad = hidden_grad * (sigma * (1.0 + pre * (1.0 - sigma)))
    contract = (((0,), (0,)), ((), ()))
    gather.phase(1)
    second = split_dot(pre * sigma, back, contract)
    first = split_dot(mean_buf[...], pre_grad, contract)
    wide = first.shape[0]
    grad_buf[0:wide] = first[:, :width] * scale
    grad_buf[wide : 2 * wide] = first[:, width:] * scale
    grad_buf[2 * wide : 3 * wide] = second * scale
    half = grad_buf.shape[0] // 2
    share = half // CHIPS
    pair = send(
        grad_buf.at[pl.ds((1 - core) * half, half)], grad_pair,
        pair_sems.at[0], pair_sems.at[1], reduce.sibling, col,
    )
    gather.phase(2)
    pair.wait_recv()
    half_buf[...] = grad_buf[pl.ds(core * half, half)] + grad_pair[...]
    grads = []
    for i, there in enumerate(reduce.rows):
        grads.append(
            send(
                half_buf.at[pl.ds(lax.div(there, 2) * share, share)], grad_in.at[i],
                grad_send.at[i], grad_recv.at[i], there, col,
            )
        )
    gather.phase(3)
    gather.phase(4)
    total = half_buf[pl.ds(lax.div(row, 2) * share, share)]
    for i, copy in enumerate(grads):
        copy.wait_recv()
        total = total + grad_in[i]
    share_ref[...] = total.astype(BF16)
    reduce.drain()
    gather.drain()
    for copy in list(backs.values()) + [back_far, pair] + grads:
        copy.wait_send()
    own.wait()


def middle(px, pb, w1, w2, scale):
    edge, wide = px.shape[1:]
    width = pb.shape[2]
    nodes = 2 * edge
    grad_rows = 3 * wide
    share = grad_rows // ROW
    return pl.pallas_call(
        functools.partial(middle_kernel, scale),
        out_shape=(
            jax.ShapeDtypeStruct((COL, nodes, width), BF16),
            jax.ShapeDtypeStruct((share, width), BF16),
        ),
        in_specs=[ANY, WHOLE, WHOLE, WHOLE],
        out_specs=(ANY, WHOLE),
        scratch_shapes=row_reduce_scratch(edge, wide)
        + [
            pltpu.VMEM((4, 4, nodes, width), BF16),
            pltpu.VMEM((4, 4, nodes, width), BF16),
            DMA((4, 4)), DMA((4, 4)),
            pltpu.VMEM((nodes, width), BF16),
            pltpu.VMEM((nodes, width), BF16),
            DMA((2,)),
            pltpu.VMEM((nodes, width), BF16),
            *gather_sems(4), DMA,
            pltpu.VMEM((nodes, wide), F32),
            pltpu.VMEM((nodes, wide), F32),
            pltpu.VMEM((grad_rows, width), F32),
            pltpu.VMEM((grad_rows // 2, width), F32),
            DMA((2,)),
            pltpu.VMEM((grad_rows // 2, width), F32),
            pltpu.VMEM((CHIPS - 1, share, width), F32),
            DMA((CHIPS - 1,)), DMA((CHIPS - 1,)),
        ],
        compiler_params=pltpu.CompilerParams(collective_id=1, has_side_effects=True, vmem_limit_bytes=SCOPED),
        name="middle",
    )(px, pb, w1, w2)


def last_kernel(
    ps_ref, share_ref,
    out_ref, grad_ref,
    held, pair_in, out_buf, in_buf, pair_send, pair_recv, near_send, near_recv, load_sems,
    col_in, col_send, col_recv, own_sem,
    sum_buf, row_send, row_recv, twin_send, twin_recv,
):
    row, col, core, x_lo, y, x_hi, z = where_am_i()
    reduce = RowReduce(
        ps_ref, held, pair_in, out_buf, in_buf, pair_send, pair_recv, near_send, near_recv, load_sems
    )
    cols = [lax.rem(col + k, COL) for k in range(1, COL)]
    sibling = reduce.sibling
    meet([(there, col) for there in [sibling] + reduce.rows] + [(row, there) for there in cols])
    across = []
    for k, there in enumerate(cols):
        across.append(
            send(share_ref, col_in.at[col], col_send.at[k], col_recv.at[k], row, there)
        )
    reduce.start()
    own = pltpu.make_async_copy(share_ref, col_in.at[col], own_sem)
    own.start()
    reduce.spread()
    own.wait()
    for copy in across:
        copy.wait_recv()
    total = col_in[0].astype(F32)
    for k in range(1, COL):
        total = total + col_in[k].astype(F32)
    sum_buf[...] = total
    share = share_ref.shape[0]

    def place(chip):
        return pl.ds((core * CHIPS + chip) * share, share)

    mine = place(lax.div(row, 2))
    grad_ref[mine] = total
    along = []
    for i, there in enumerate(reduce.rows):
        along.append(
            send(sum_buf, grad_ref.at[mine], row_send.at[i], row_recv.at[i], there, col)
        )
    twins = [send(sum_buf, grad_ref.at[mine], twin_send.at[7], twin_recv.at[7], sibling, col)]
    out_ref[...] = reduce.finish().reshape(out_ref.shape)
    for i, (dx, dy) in enumerate(NEAR):
        from_x = lax.rem(x_lo + dx, 2)
        from_y = lax.rem(y - dy + Y, Y)
        along[i].wait_recv()
        theirs = place(from_x * Y + from_y)
        twins.append(
            send(
                grad_ref.at[theirs], grad_ref.at[theirs],
                twin_send.at[i], twin_recv.at[i], sibling, col,
            )
        )
    for copy in twins:
        copy.wait_recv()
    reduce.drain()
    for copy in across + along + twins:
        copy.wait_send()


def last(ps, share):
    edge, width = ps.shape[1:]
    return pl.pallas_call(
        last_kernel,
        out_shape=(
            jax.ShapeDtypeStruct((2 * edge, width), F32),
            jax.ShapeDtypeStruct((ROW * share.shape[0], width), F32),
        ),
        in_specs=[ANY, WHOLE],
        out_specs=(WHOLE, WHOLE),
        scratch_shapes=row_reduce_scratch(edge, width)
        + [
            pltpu.VMEM((COL,) + share.shape, BF16),
            DMA((COL - 1,)), DMA((COL - 1,)), DMA,
            pltpu.VMEM(share.shape, F32),
            DMA((7,)), DMA((7,)), DMA((8,)), DMA((8,)),
        ],
        compiler_params=pltpu.CompilerParams(collective_id=2, has_side_effects=True, vmem_limit_bytes=SCOPED),
        name="last",
    )(ps, share)


def arrange_kernel(out_ref, grad_ref, output_ref, first_ref, second_ref):
    wide = first_ref.shape[0]
    width = second_ref.shape[1]
    output_ref[...] = out_ref[...].astype(BF16)
    first_ref[:, :width] = grad_ref[:wide]
    first_ref[:, width:] = grad_ref[wide : 2 * wide]
    second_ref[...] = grad_ref[2 * wide :]


def arrange(out, grads, wide):
    return pl.pallas_call(
        arrange_kernel,
        out_shape=(
            jax.ShapeDtypeStruct(out.shape, BF16),
            jax.ShapeDtypeStruct((wide, 2 * grads.shape[1]), F32),
            jax.ShapeDtypeStruct((wide, grads.shape[1]), F32),
        ),
        in_specs=[WHOLE, WHOLE],
        out_specs=(WHOLE, WHOLE, WHOLE),
        compiler_params=pltpu.CompilerParams(vmem_limit_bytes=SCOPED),
        name="arrange",
    )(out, grads)


def in_hbm(array):
    return pltpu.with_memory_space_constraint(array, pltpu.HBM)


def on_device(
    node_features, tile_values, tile_coords, tile_counts, first_weight, second_weight, out_grad
):
    edge = tile_values.shape[-1]
    slots = tile_values.shape[2]
    tiles = tile_values.reshape(slots, edge, edge)
    coords = in_hbm(tile_coords.reshape(slots, 2).T)
    count = tile_counts.reshape(1)
    scale = 1.0 / math.sqrt(node_features.shape[0] * ROW * COL)
    gx, gg, tiles = gather_inputs(in_hbm(node_features), in_hbm(out_grad), in_hbm(tiles))
    px, pb = propagate(
        both_kernel, coords, count, tiles,
        [gx.reshape(-1, edge, gx.shape[-1]), gg.reshape(-1, edge, gg.shape[-1])], "both",
    )
    gh, share = middle(px, pb, first_weight, second_weight, scale)
    (ps,) = propagate(
        one_kernel, coords, count, tiles, [gh.reshape(-1, edge, gh.shape[-1])], "one"
    )
    out, grads = last(ps, share)
    return arrange(out, grads, first_weight.shape[0])


def solution(mesh):
    return jax.shard_map(
        on_device,
        mesh=mesh,
        in_specs=(
            P(("row", "col"), None),
            P("row", "col", None, None, None),
            P("row", "col", None, None),
            P("row", "col"),
            P(),
            P(),
            P(("row", "col"), None),
        ),
        out_specs=(P(("row", "col"), None), P(), P()),
        check_vma=False,
    )
```
